128 devices in a mesh: row: 8 (over x, core), col: 16 (over z, y).
Axes of the slice: x: 4, y: 4, z: 4, core: 2. Of those that a mesh axis runs over, the one named last changes fastest.
Arguments:
- moment_x: float32 [496, 496], P('row', 'col'), may hold values from -8 to 8
- zinv: float32 [496, 496], P('row', 'col'), may hold values from -8 to 8
- positions: int32 [4096, 16], P(('row', 'col')), may hold values from 0 to 495
- entry_count: int32 [4096], P(('row', 'col')), may hold values from 1 to 8
Outputs:
- schur: float32 [4096, 4096], P('row', 'col')
The draws below stay inside these ranges and needn't reach their ends.
All inputs are finite; a program needn't handle non-finite values.
Results may differ from the reference program's by a relative error of at most 0.0003.
Values sent between devices are 32-bit elements; how exact they have to be, the bound alone decides.
A program may use at most 64 MiB of HBM per device.

```python
import jax
import jax.numpy as jnp
from jax import lax

NMON = 496
SLOTS = 8
CONS = 4096


def symmetric_draw(key):
    key_a = jax.random.fold_in(key, 11)
    key_s = jax.random.fold_in(key, 23)
    base = jax.random.normal(key_a, (NMON, NMON), jnp.float32)
    scales = jnp.exp(jax.random.uniform(key_s, (NMON,), jnp.float32, -0.5, 0.47))
    mixed = 0.5 * (base + base.T) * scales[:, None] * scales[None, :]
    return jnp.clip(mixed, -8.0, 8.0)


def draw_moment_x(key, part):
    return symmetric_draw(jax.random.fold_in(key, 101))


def draw_zinv(key, part):
    return symmetric_draw(jax.random.fold_in(key, 202))


def set_ends(array, own_key, low, top_value):
    spot = [jax.random.randint(jax.random.fold_in(own_key, axis), (), 0, length) for axis, length in enumerate(array.shape)]
    main_axis = array.shape.index(max(array.shape))
    next_to = spot[:main_axis] + [(spot[main_axis] + 1) % array.shape[main_axis]] + spot[main_axis + 1:]
    return array.at[tuple(spot)].set(low).at[tuple(next_to)].set(top_value)


def setup_inputs(seed: int = 0) -> dict:
    key_list = jax.random.split(jax.random.key(seed), 5)
    moment_x = draw_moment_x(jax.random.fold_in(key_list[4], 71), 0)
    zinv = draw_zinv(jax.random.fold_in(key_list[4], 71), 0)
    positions = set_ends(jax.random.randint(key_list[2], (CONS, 2 * SLOTS), 0, NMON), jax.random.fold_in(key_list[2], 1), 0, NMON - 1).astype(jnp.int32)
    entry_count = set_ends(jax.random.randint(key_list[3], (CONS,), 1, SLOTS + 1), jax.random.fold_in(key_list[3], 1), 1, SLOTS).astype(jnp.int32)
    return dict(moment_x=moment_x, zinv=zinv, positions=positions, entry_count=entry_count)


def schur_rows(moment_x, zinv, row_positions, row_counts, col_positions, col_counts, group_rows):
    slot_count = row_positions.shape[1] // 2
    slot_iota = jnp.arange(slot_count, dtype=jnp.int32)
    col_left = col_positions[:, :slot_count].reshape(-1)
    col_right = col_positions[:, slot_count:].reshape(-1)
    col_alive = (slot_iota[None, :] < col_counts[:, None]).astype(jnp.float32).reshape(-1)
    ncols = col_positions.shape[0]
    nrows = row_positions.shape[0]

    def one_group(packed):
        grp_positions, grp_counts = packed
        grp_left = grp_positions[:, :slot_count].reshape(-1)
        grp_right = grp_positions[:, slot_count:].reshape(-1)
        grp_alive = (slot_iota[None, :] < grp_counts[:, None]).astype(jnp.float32).reshape(-1)
        x_picked = jnp.take(jnp.take(moment_x, grp_right, axis=0), col_left, axis=1)
        w_picked = jnp.take(jnp.take(zinv, col_right, axis=0), grp_left, axis=1)
        terms = x_picked * w_picked.T * grp_alive[:, None] * col_alive[None, :]
        return jnp.sum(terms.reshape(group_rows, slot_count, ncols, slot_count), axis=(1, 3))

    grouped = (row_positions.reshape(nrows // group_rows, group_rows, 2 * slot_count),
               row_counts.reshape(nrows // group_rows, group_rows))
    return lax.map(one_group, grouped).reshape(nrows, ncols)


def reference(moment_x, zinv, positions, entry_count):
    return schur_rows(moment_x, zinv, positions, entry_count, positions, entry_count, 64)
```

```python
import functools

import jax
import jax.numpy as jnp
from jax import lax
from jax.experimental import pallas as pl
from jax.experimental.pallas import tpu as pltpu
from jax.sharding import PartitionSpec as P

MESH = pl.DeviceIdType.MESH
F32 = jnp.float32
BF16 = jnp.bfloat16
I32 = jnp.int32


def padded(v):
    return v + lax.shift_right_logical(v * 2115, 16)


def gather_kernel(x_ref, w_ref, pos_ref, cnt_ref, g_ref, gi_ref, slab, islab, send, recv, isend, irecv, psend, precv, loc):
    r = lax.axis_index("row")
    c = lax.axis_index("col")
    xx = r // 2
    core = r % 2
    zz = c // 4
    yy = c % 4
    me = 16 * r + c

    def peer(n):
        dx, dz, dy = n // 16, (n // 4) % 4, n % 4
        return (2 * ((xx + dx) % 4) + core, 4 * ((zz + dz) % 4) + (yy + dy) % 4)

    barrier = pltpu.get_barrier_semaphore()

    def greet(n, carry):
        pl.semaphore_signal(barrier, inc=1, device_id=peer(n), device_id_type=MESH)
        return carry

    lax.fori_loop(1, 64, greet, 0)
    partner = (r + 1 - 2 * core, c)
    pl.semaphore_signal(barrier, inc=1, device_id=partner, device_id_type=MESH)

    slab[...] = jnp.zeros_like(slab)
    slab[0:31, 0:31] = x_ref[0:31, :]
    slab[0:31, 32:63] = x_ref[31:62, :]
    slab[0:31, 64:95] = w_ref[0:31, :]
    slab[0:31, 96:127] = w_ref[31:62, :]

    post = jnp.transpose(pos_ref[...])
    slot = lax.broadcasted_iota(I32, (16, 32), 0) % 8
    live = slot < cnt_ref[...].reshape(1, 32)
    post = jnp.where(live, padded(post), 31)
    rows = jnp.transpose(post) * 8
    islab[...] = jnp.zeros_like(islab)
    for u in range(4):
        islab[:, 16 * u : 16 * u + 16] = rows[8 * u : 8 * u + 8, :]
    islab[:, 64:96] = post[0:8, :]
    islab[:, 96:128] = post[8:16, :]

    own = pltpu.make_async_copy(slab, g_ref.at[me], loc.at[0])
    iown = pltpu.make_async_copy(islab, gi_ref.at[me], loc.at[1])
    own.start()
    iown.start()
    pl.semaphore_wait(barrier, 64)

    def send_one(n, carry):
        to = peer(n)
        dx = n // 16
        pltpu.make_async_remote_copy(
            islab, gi_ref.at[me], isend, irecv.at[dx], device_id=to, device_id_type=MESH
        ).start()
        pltpu.make_async_remote_copy(
            slab, g_ref.at[me], send, recv.at[dx], device_id=to, device_id_type=MESH
        ).start()
        return carry

    lax.fori_loop(1, 64, send_one, 0)
    own.wait()
    iown.wait()

    for d in range(4):
        count = 15 if d == 0 else 16
        pltpu.make_async_copy(g_ref.at[0:count], g_ref.at[0:count], recv.at[d]).wait()
        pltpu.make_async_copy(gi_ref.at[0:count], gi_ref.at[0:count], irecv.at[d]).wait()
        src = 16 * (2 * ((xx + 4 - d) % 4) + core)
        pltpu.make_async_remote_copy(
            g_ref.at[pl.ds(src, 16)], g_ref.at[pl.ds(src, 16)], psend.at[0], precv.at[0],
            device_id=partner, device_id_type=MESH,
        ).start()
        pltpu.make_async_remote_copy(
            gi_ref.at[pl.ds(src, 16)], gi_ref.at[pl.ds(src, 16)], psend.at[1], precv.at[1],
            device_id=partner, device_id_type=MESH,
        ).start()
    pltpu.make_async_copy(g_ref.at[0:63], g_ref.at[0:63], send).wait()
    pltpu.make_async_copy(gi_ref.at[0:63], gi_ref.at[0:63], isend).wait()
    for sems in (psend, precv):
        pltpu.make_async_copy(g_ref.at[0:64], g_ref.at[0:64], sems.at[0]).wait()
        pltpu.make_async_copy(gi_ref.at[0:64], gi_ref.at[0:64], sems.at[1]).wait()


def table_kernel(g_ref, gi_ref, out_ref, sm, ci, xh, wh, tx0, tx1, tw0, tw1, pq, sem):
    r = lax.axis_index("row")
    c = lax.axis_index("col")
    rows_in = pltpu.make_async_copy(gi_ref.at[pl.ds(16 * r, 16)], sm, sem.at[0])
    rows_in.start()
    cols_in = pltpu.make_async_copy(gi_ref.at[pl.ds(8 * c, 8)], ci, sem.at[1])
    cols_in.start()

    lane = lax.broadcasted_iota(I32, (32, 128), 1)

    def assemble(rr, carry):
        for z in range(4):
            parts = [g_ref[16 * rr + 4 * z + y] for y in range(4)]
            for g in range(4):
                full = None
                for y in range(4):
                    turned = parts[y] if y == g else pltpu.roll(parts[y], (32 * (y - g)) % 128, 1)
                    full = turned if full is None else jnp.where(lane >= 32 * y, turned, full)
                hi = full.astype(BF16)
                lo = (full - hi.astype(F32)).astype(BF16)
                to = xh if g < 2 else wh
                at = pl.ds(pl.multiple_of(64 * rr + 32 * (g % 2), 32), 32)
                to[at, 128 * z : 128 * z + 128] = hi
                to[at, 512 + 128 * z : 640 + 128 * z] = lo
        return carry

    lax.fori_loop(0, 8, assemble, 0)
    cols_in.wait()
    lane8 = lax.broadcasted_iota(I32, (8, 128), 1)
    for half in range(2):
        for which in range(2):
            full = None
            for y in range(4):
                t = pltpu.roll(ci[4 * half + y], (32 * (y - 2 - which)) % 128, 1)
                full = t if full is None else jnp.where(lane8 >= 32 * y, t, full)
            pq[8 * which : 8 * which + 8, 128 * half : 128 * half + 128] = full

    place = lax.broadcasted_iota(I32, (512, 256), 0)

    def tables(l, carry):
        for which, half_ref, t0, t1 in ((0, xh, tx0, tx1), (1, wh, tw0, tw1)):
            picked = pq[pl.ds(8 * which + l, 1), :]
            hot = jnp.where(place == picked, 1.0, 0.0).astype(BF16)
            t = jnp.dot(half_ref[:, 0:512], hot, preferred_element_type=F32)
            t = t + jnp.dot(half_ref[:, 512:1024], hot, preferred_element_type=F32)
            t0[pl.ds(l, 512, stride=8), :] = t[:, 0:128]
            t1[pl.ds(l, 512, stride=8), :] = t[:, 128:256]
        return carry

    lax.fori_loop(0, 8, tables, 0)
    rows_in.wait()

    sub = lax.broadcasted_iota(I32, (8, 128), 0)
    low4, low2, low1 = sub < 4, sub % 4 < 2, sub % 2 < 1

    def folded(a):
        b = [
            jnp.where(low4, a[v], a[v + 4]) + pltpu.roll(jnp.where(low4, a[v + 4], a[v]), 4, 0)
            for v in range(4)
        ]
        d = [
            jnp.where(low2, b[v], pltpu.roll(b[v + 2], 2, 0))
            + jnp.where(low2, pltpu.roll(b[v], 6, 0), b[v + 2])
            for v in range(2)
        ]
        return jnp.where(low1, d[0], pltpu.roll(d[1], 1, 0)) + jnp.where(
            low1, pltpu.roll(d[0], 7, 0), d[1]
        )

    def group(n, carry):
        m, u = n // 4, n % 4
        left, right = [], []
        for v in range(8):
            a0, a1 = None, None
            for k in range(8):
                p = pl.multiple_of(sm[m, v, 16 * u + k], 8)
                q = pl.multiple_of(sm[m, v, 16 * u + 8 + k], 8)
                s0 = tx0[pl.ds(q, 8), :] * tw0[pl.ds(p, 8), :]
                s1 = tx1[pl.ds(q, 8), :] * tw1[pl.ds(p, 8), :]
                a0 = s0 if a0 is None else a0 + s0
                a1 = s1 if a1 is None else a1 + s1
            left.append(a0)
            right.append(a1)
        at = pl.ds(pl.multiple_of(8 * n, 8), 8)
        out_ref[at, 0:128] = folded(left)
        out_ref[at, 128:256] = folded(right)
        return carry

    lax.fori_loop(0, 64, group, 0)


def gather(x, w, pos, cnt):
    dma = pltpu.SemaphoreType.DMA
    return pl.pallas_call(
        gather_kernel,
        out_shape=(
            jax.ShapeDtypeStruct((128, 32, 128), F32),
            jax.ShapeDtypeStruct((128, 8, 128), I32),
        ),
        in_specs=[pl.BlockSpec(memory_space=pltpu.VMEM)] * 4,
        out_specs=(pl.BlockSpec(memory_space=pl.ANY), pl.BlockSpec(memory_space=pl.ANY)),
        scratch_shapes=[
            pltpu.VMEM((32, 128), F32),
            pltpu.VMEM((8, 128), I32),
            dma,
            dma((4,)),
            dma,
            dma((4,)),
            dma((2,)),
            dma((2,)),
            dma((2,)),
        ],
        compiler_params=pltpu.CompilerParams(collective_id=0, has_side_effects=True),
        name="gather",
    )(x, w, pos, cnt)


def tabled(g, gi):
    table = pltpu.VMEM((4096, 128), F32)
    return pl.pallas_call(
        table_kernel,
        out_shape=jax.ShapeDtypeStruct((512, 256), F32),
        in_specs=[pl.BlockSpec(memory_space=pltpu.VMEM), pl.BlockSpec(memory_space=pl.ANY)],
        out_specs=pl.BlockSpec(memory_space=pltpu.VMEM),
        scratch_shapes=[
            pltpu.SMEM((16, 8, 128), I32),
            pltpu.VMEM((8, 8, 128), I32),
            pltpu.VMEM((512, 1024), BF16),
            pltpu.VMEM((512, 1024), BF16),
            table,
            table,
            table,
            table,
            pltpu.VMEM((16, 256), I32),
            pltpu.SemaphoreType.DMA((2,)),
        ],
        compiler_params=pltpu.CompilerParams(vmem_limit_bytes=48 << 20),
        name="tables",
    )(g, gi)


def shards(moment_x, zinv, positions, entry_count):
    g, gi = gather(moment_x, zinv, positions, entry_count)
    return tabled(g, gi)


def solution(mesh):
    return jax.shard_map(
        shards,
        mesh=mesh,
        in_specs=(P("row", "col"), P("row", "col"), P(("row", "col"), None), P(("row", "col"))),
        out_specs=P("row", "col"),
        check_vma=False,
    )
```

```python
import functools

import jax
import jax.numpy as jnp
from jax import lax
from jax.experimental import pallas as pl
from jax.experimental.pallas import tpu as pltpu
from jax.sharding import PartitionSpec as P

MESH = pl.DeviceIdType.MESH
F32 = jnp.float32
BF16 = jnp.bfloat16
I32 = jnp.int32


def padded(v, part, factor, pad):
    return v + pad * lax.shift_right_logical(v * factor, 16)


def gather_kernel(
    x_in, w_in, pos_in, cnt_in, ga, gb, gc,
    x_ref, w_ref, pos_ref, cnt_ref, slab_a, slab_b, slab_c, loc, s1, s2, s3, sp, r1, r2, r3, rp,
):
    r = lax.axis_index("row")
    c = lax.axis_index("col")
    core = r % 2
    here = (r // 2, c // 4, c % 4)
    ins = [
        pltpu.make_async_copy(a, b, loc.at[n])
        for n, (a, b) in enumerate(((x_in, x_ref), (w_in, w_ref), (pos_in, pos_ref), (cnt_in, cnt_ref)))
    ]
    for copy in ins:
        copy.start()

    def moved(axis, offset):
        at = list(here)
        at[axis] = (at[axis] + offset) % 4
        return at

    def device(at):
        return (2 * at[0] + core, 4 * at[1] + at[2])

    partner = (r + 1 - 2 * core, c)
    barrier = pltpu.get_barrier_semaphore()
    for axis in range(3):
        for offset in (1, 3, 2):
            pl.semaphore_signal(barrier, inc=1, device_id=device(moved(axis, offset)), device_id_type=MESH)
    pl.semaphore_signal(barrier, inc=1, device_id=partner, device_id_type=MESH)

    for ref in (slab_a, slab_b, slab_c):
        ref[...] = jnp.zeros_like(ref)
    for copy in ins:
        copy.wait()
    for lanes, src in ((0, x_ref), (64, w_ref)):
        slab_a[:, lanes : lanes + 62] = src[0:16, :]
        slab_b[0:8, lanes : lanes + 62] = src[16:24, :]
        slab_c[0:7, lanes : lanes + 62] = src[24:31, :]

    pos = pos_ref[...]
    live = lax.broadcasted_iota(I32, (16, 32), 0) % 8 < cnt_ref[...].reshape(1, 32)
    cols = jnp.where(live, padded(pos, 62, 1058, 2), 62).astype(F32)
    rows = jnp.where(live, padded(pos, 31, 2115, 1), 31).astype(F32) * 8.0
    rows = jnp.transpose(rows)
    for u in range(4):
        slab_b[8:16, 16 * u : 16 * u + 16] = rows[8 * u : 8 * u + 8, :]
    slab_b[8:16, 64:96] = cols[0:8, :]
    slab_b[8:16, 96:128] = cols[8:16, :]

    every = pl.ds(0, 4)
    parts = ((ga, slab_a, (0, 2, 1)), (gb, slab_b, (2, 1, 0)), (gc, slab_c, (1, 0, 2)))

    def box(g, at, open_axes=()):
        index = [every if axis in open_axes else at[axis] for axis in range(3)]
        return g.at[index[0], core, index[1], index[2]]

    own = [
        pltpu.make_async_copy(slab, box(g, here), loc.at[4 + n]) for n, (g, slab, order) in enumerate(parts)
    ]
    for copy in own:
        copy.start()
    pl.semaphore_wait(barrier, 10)

    def send(src, dst, send_sem, recv_sem, to):
        pltpu.make_async_remote_copy(
            src, dst, send_sem, recv_sem, device_id=to, device_id_type=MESH
        ).start()

    def wait(ref, sem):
        pltpu.make_async_copy(ref, ref, sem).wait()

    for n, (g, slab, order) in enumerate(parts):
        for offset in (1, 3, 2):
            send(slab, box(g, here), s1.at[n], r1.at[n], device(moved(order[0], offset)))
    for copy in own:
        copy.wait()
    for n, (g, slab, order) in enumerate(parts):
        wait(g.at[0, 0, 0, 0:3], r1.at[n])
        line = box(g, here, order[:1])
        for offset in (1, 3, 2):
            send(line, line, s2.at[n], r2.at[n, offset - 1], device(moved(order[1], offset)))
        for offset in (1, 3, 2):
            send(line, line, s3.at[n], r3.at[n, offset - 1], device(moved(order[2], offset)))
    for back in (1, 3, 2):
        for n, (g, slab, order) in enumerate(parts):
            wait(g.at[0, 0, 0, 0:4], r2.at[n, back - 1])
            line = box(g, moved(order[1], 4 - back), order[:1])
            for offset in (1, 3, 2):
                send(line, line, s3.at[n], r3.at[n, offset - 1], device(moved(order[2], offset)))
    for n, (g, slab, order) in enumerate(parts):
        plane = box(g, here, order[:2])
        send(plane, plane, sp.at[n], rp.at[n], partner)
    for back in (1, 3, 2):
        for n, (g, slab, order) in enumerate(parts):
            wait(g.at[0, 0], r3.at[n, back - 1])
            plane = box(g, moved(order[2], 4 - back), order[:2])
            send(plane, plane, sp.at[n], rp.at[n], partner)
    for n, (g, slab, order) in enumerate(parts):
        wait(g.at[0, 0, 0, 0:3], s1.at[n])
        wait(g.at[0, 0, 0:3], s2.at[n])
        wait(g.at[0:3, 0], s3.at[n])
        wait(g.at[:, 0], sp.at[n])
        wait(g.at[:, 0], rp.at[n])


def table_kernel(ga_ref, gb_ref, gc_ref, out_ref, sm, flat, xh, tx, pq, sem, acc):
    r = lax.axis_index("row")
    c = lax.axis_index("col")

    lane16 = lax.broadcasted_iota(I32, (16, 128), 1)
    by_row = [gb_ref[pl.ds(256 * r + 8 + v, 16, stride=16), :] for v in range(8)]
    for u in range(4):
        full = None
        for v in range(8):
            turn = (16 * (v - u)) % 128
            t = by_row[v] if turn == 0 else pltpu.roll(by_row[v], turn, 1)
            full = t if full is None else jnp.where(lane16 >= 16 * v, t, full)
        flat[pl.ds(u, 16, stride=4), :] = full.astype(I32)
    to_scalar = pltpu.make_async_copy(flat, sm, sem)
    to_scalar.start()

    lane8 = lax.broadcasted_iota(I32, (8, 128), 1)
    for half in range(2):
        for which in range(2):
            full = None
            for y in range(4):
                tile = gb_ref[pl.ds(pl.multiple_of(16 * (8 * c + 4 * half + y) + 8, 8), 8), :]
                turn = (32 * (y - 2 - which)) % 128
                t = tile if turn == 0 else pltpu.roll(tile, turn, 1)
                full = t if full is None else jnp.where(lane8 >= 32 * y, t, full)
            pq[8 * which : 8 * which + 8, 128 * half : 128 * half + 128] = full.astype(I32)

    left = lane16 < 64

    def assemble(cc, carry):
        for xx in range(4):
            even, odd = 32 * xx + cc, 32 * xx + 16 + cc
            tops = [ga_ref[pl.ds(pl.multiple_of(16 * d, 16), 16), :] for d in (even, odd)]
            lows = [
                jnp.concatenate(
                    [
                        gb_ref[pl.ds(pl.multiple_of(16 * d, 16), 8), :],
                        gc_ref[pl.ds(pl.multiple_of(8 * d, 8), 8), :],
                    ],
                    axis=0,
                )
                for d in (even, odd)
            ]
            for low, (a, b) in enumerate((tops, lows)):
                for which in range(2):
                    if which == 0:
                        full = jnp.where(left, a, pltpu.roll(b, 64, 1))
                    else:
                        full = jnp.where(left, pltpu.roll(a, 64, 1), b)
                    hi = full.astype(BF16)
                    lo = (full - hi.astype(F32)).astype(BF16)
                    at = pl.ds(pl.multiple_of(512 * which + 32 * cc + 16 * low, 16), 16)
                    xh[at, 128 * xx : 128 * xx + 128] = hi
                    xh[at, 512 + 128 * xx : 640 + 128 * xx] = lo
        return carry

    lax.fori_loop(0, 16, assemble, 0)

    place = lax.broadcasted_iota(I32, (512, 256), 0)

    def tables(n, carry):
        which, l = n // 8, n % 8
        picked = pq[pl.ds(n, 1), :]
        hot = jnp.where(place == picked, 1.0, 0.0).astype(BF16)
        t = jnp.dot(
            xh[pl.ds(pl.multiple_of(512 * which, 512), 512), :],
            jnp.concatenate([hot, hot], axis=0),
            preferred_element_type=F32,
        )
        tx[pl.ds(8192 * which + l, 512, stride=8), :] = t[:, 0:128]
        tx[pl.ds(8192 * which + 4096 + l, 512, stride=8), :] = t[:, 128:256]
        return carry

    lax.fori_loop(0, 16, tables, 0)
    to_scalar.wait()

    sub = lax.broadcasted_iota(I32, (8, 128), 0)
    low4, low2, low1 = sub < 4, sub % 4 < 2, sub % 2 < 1

    def folded(a):
        b = [
            jnp.where(low4, a[v], a[v + 4]) + pltpu.roll(jnp.where(low4, a[v + 4], a[v]), 4, 0)
            for v in range(4)
        ]
        d = [
            jnp.where(low2, b[v], pltpu.roll(b[v + 2], 2, 0))
            + jnp.where(low2, pltpu.roll(b[v], 6, 0), b[v + 2])
            for v in range(2)
        ]
        return jnp.where(low1, d[0], pltpu.roll(d[1], 1, 0)) + jnp.where(
            low1, pltpu.roll(d[0], 7, 0), d[1]
        )

    def fold_group(n, slot):
        at = pl.ds(pl.multiple_of(8 * n, 8), 8)
        for half in range(2):
            here = [acc[pl.ds(pl.multiple_of(128 * slot + 64 * half + 8 * v, 8), 8), :] for v in range(8)]
            out_ref[at, 128 * half : 128 * half + 128] = folded(here)

    def group(n, carry):
        slot = n % 2
        fold_group(jnp.maximum(n - 1, 0), 1 - slot)
        for v in range(8):
            a0, a1 = None, None
            for k in range(8):
                p = pl.multiple_of(sm[n, 16 * v + k], 8)
                q = pl.multiple_of(sm[n, 16 * v + 8 + k], 8)
                s0 = tx[pl.ds(q, 8), :] * tx[pl.ds(p + 8192, 8), :]
                s1 = tx[pl.ds(q + 4096, 8), :] * tx[pl.ds(p + 12288, 8), :]
                a0 = s0 if a0 is None else a0 + s0
                a1 = s1 if a1 is None else a1 + s1
            acc[pl.ds(pl.multiple_of(128 * slot + 8 * v, 8), 8), :] = a0
            acc[pl.ds(pl.multiple_of(128 * slot + 64 + 8 * v, 8), 8), :] = a1
        return carry

    lax.fori_loop(0, 64, group, 0)
    fold_group(63, 1)


def gather(x, w, pos, cnt):
    dma = pltpu.SemaphoreType.DMA
    return pl.pallas_call(
        gather_kernel,
        out_shape=tuple(jax.ShapeDtypeStruct((4, 2, 4, 4, n, 128), F32) for n in (16, 16, 8)),
        in_specs=[pl.BlockSpec(memory_space=pl.ANY)] * 4,
        out_specs=tuple(pl.BlockSpec(memory_space=pl.ANY) for n in range(3)),
        scratch_shapes=[
            pltpu.VMEM((31, 62), F32),
            pltpu.VMEM((31, 62), F32),
            pltpu.VMEM((16, 32), I32),
            pltpu.VMEM((32,), I32),
            pltpu.VMEM((16, 128), F32),
            pltpu.VMEM((16, 128), F32),
            pltpu.VMEM((8, 128), F32),
            dma((7,)),
            dma((3,)),
            dma((3,)),
            dma((3,)),
            dma((3,)),
            dma((3,)),
            dma((3, 3)),
            dma((3, 3)),
            dma((3,)),
        ],
        compiler_params=pltpu.CompilerParams(collective_id=0, has_side_effects=True),
        name="gather",
    )(x, w, pos, cnt)


def tabled(ga, gb, gc):
    return pl.pallas_call(
        table_kernel,
        out_shape=jax.ShapeDtypeStruct((512, 256), F32),
        in_specs=[pl.BlockSpec(memory_space=pltpu.VMEM)] * 3,
        out_specs=pl.BlockSpec(memory_space=pltpu.VMEM),
        scratch_shapes=[
            pltpu.SMEM((64, 128), I32),
            pltpu.VMEM((64, 128), I32),
            pltpu.VMEM((1024, 1024), BF16),
            pltpu.VMEM((16384, 128), F32),
            pltpu.VMEM((16, 256), I32),
            pltpu.SemaphoreType.DMA,
            pltpu.VMEM((256, 128), F32),
        ],
        compiler_params=pltpu.CompilerParams(vmem_limit_bytes=48 << 20),
        name="tables",
    )(ga, gb, gc)


def shards(moment_x, zinv, positions, entry_count):
    g = gather(moment_x.T, zinv.T, positions.T, entry_count)
    return tabled(*(a.reshape(-1, 128) for a in g))


def solution(mesh):
    return jax.shard_map(
        shards,
        mesh=mesh,
        in_specs=(P("row", "col"), P("row", "col"), P(("row", "col"), None), P(("row", "col"))),
        out_specs=P("row", "col"),
        check_vma=False,
    )
```

```python
import functools

import jax
import jax.numpy as jnp
from jax import lax
from jax.experimental import pallas as pl
from jax.experimental.pallas import tpu as pltpu
from jax.sharding import PartitionSpec as P

MESH = pl.DeviceIdType.MESH
F32 = jnp.float32
BF16 = jnp.bfloat16
I32 = jnp.int32


def padded(v, part, factor, pad):
    return v + pad * lax.shift_right_logical(v * factor, 16)


def gather_kernel(
    x_in, w_in, pos_in, cnt_in, ga, gb, gc,
    x_ref, w_ref, pos_ref, cnt_ref, slab_a, slab_b, slab_c, loc, s1, s2, s3, sp, r1, r2, r3, rp,
):
    r = lax.axis_index("row")
    c = lax.axis_index("col")
    core = r % 2
    here = (r // 2, c // 4, c % 4)
    ins = [
        pltpu.make_async_copy(a, b, loc.at[n])
        for n, (a, b) in enumerate(((x_in, x_ref), (w_in, w_ref), (pos_in, pos_ref), (cnt_in, cnt_ref)))
    ]
    for copy in ins:
        copy.start()

    def moved(axis, offset):
        at = list(here)
        at[axis] = (at[axis] + offset) % 4
        return at

    def device(at):
        return (2 * at[0] + core, 4 * at[1] + at[2])

    partner = (r + 1 - 2 * core, c)
    barrier = pltpu.get_barrier_semaphore()
    for axis in range(3):
        for offset in (1, 3, 2):
            pl.semaphore_signal(barrier, inc=1, device_id=device(moved(axis, offset)), device_id_type=MESH)
    pl.semaphore_signal(barrier, inc=1, device_id=partner, device_id_type=MESH)

    for ref in (slab_a, slab_b, slab_c):
        ref[...] = jnp.zeros_like(ref)
    for copy in ins:
        copy.wait()
    for lanes, src in ((0, x_ref), (64, w_ref)):
        slab_a[:, lanes : lanes + 62] = src[0:16, :]
        slab_b[0:8, lanes : lanes + 62] = src[16:24, :]
        slab_c[0:7, lanes : lanes + 62] = src[24:31, :]

    pos = pos_ref[...]
    live = lax.broadcasted_iota(I32, (16, 32), 0) % 8 < cnt_ref[...].reshape(1, 32)
    cols = jnp.where(live, padded(pos, 62, 1058, 2), 62).astype(F32)
    rows = jnp.where(live, padded(pos, 31, 2115, 1), 31).astype(F32) * 16.0
    rows = jnp.transpose(rows)
    for u in range(4):
        slab_b[8:16, 16 * u : 16 * u + 16] = rows[8 * u : 8 * u + 8, :]
    slab_b[8:16, 64:96] = cols[0:8, :]
    slab_b[8:16, 96:128] = cols[8:16, :]

    every = pl.ds(0, 4)
    parts = ((ga, slab_a, (0, 2, 1)), (gb, slab_b, (2, 1, 0)), (gc, slab_c, (1, 0, 2)))

    def box(g, at, open_axes=()):
        index = [every if axis in open_axes else at[axis] for axis in range(3)]
        return g.at[index[0], core, index[1], index[2]]

    own = [
        pltpu.make_async_copy(slab, box(g, here), loc.at[4 + n]) for n, (g, slab, order) in enumerate(parts)
    ]
    for copy in own:
        copy.start()
    pl.semaphore_wait(barrier, 10)

    def send(src, dst, send_sem, recv_sem, to):
        pltpu.make_async_remote_copy(
            src, dst, send_sem, recv_sem, device_id=to, device_id_type=MESH
        ).start()

    def wait(ref, sem):
        pltpu.make_async_copy(ref, ref, sem).wait()

    for n, (g, slab, order) in enumerate(parts):
        for offset in (1, 3, 2):
            send(slab, box(g, here), s1.at[n], r1.at[n], device(moved(order[0], offset)))
    for copy in own:
        copy.wait()
    for n, (g, slab, order) in enumerate(parts):
        wait(g.at[0, 0, 0, 0:3], r1.at[n])
        line = box(g, here, order[:1])
        for offset in (1, 3, 2):
            send(line, line, s2.at[n], r2.at[n, offset - 1], device(moved(order[1], offset)))
        for offset in (1, 3, 2):
            send(line, line, s3.at[n], r3.at[n, offset - 1], device(moved(order[2], offset)))
    for back in (1, 3, 2):
        for n, (g, slab, order) in enumerate(parts):
            wait(g.at[0, 0, 0, 0:4], r2.at[n, back - 1])
            line = box(g, moved(order[1], 4 - back), order[:1])
            for offset in (1, 3, 2):
                send(line, line, s3.at[n], r3.at[n, offset - 1], device(moved(order[2], offset)))
    for n, (g, slab, order) in enumerate(parts):
        plane = box(g, here, order[:2])
        send(plane, plane, sp.at[n], rp.at[n], partner)
    for back in (1, 3, 2):
        for n, (g, slab, order) in enumerate(parts):
            wait(g.at[0, 0], r3.at[n, back - 1])
            plane = box(g, moved(order[2], 4 - back), order[:2])
            send(plane, plane, sp.at[n], rp.at[n], partner)
    for n, (g, slab, order) in enumerate(parts):
        wait(g.at[0, 0, 0, 0:3], s1.at[n])
        wait(g.at[0, 0, 0:3], s2.at[n])
        wait(g.at[0:3, 0], s3.at[n])
        wait(g.at[:, 0], sp.at[n])
        wait(g.at[:, 0], rp.at[n])


def table_kernel(ga_ref, gb_ref, gc_ref, out_ref, sm, flat, xh, tx, pq, sem, acc):
    r = lax.axis_index("row")
    c = lax.axis_index("col")

    lane16 = lax.broadcasted_iota(I32, (16, 128), 1)
    by_row = [gb_ref[pl.ds(256 * r + 8 + v, 16, stride=16), :] for v in range(8)]
    for u in range(4):
        full = None
        for v in range(8):
            turn = (16 * (v - u)) % 128
            t = by_row[v] if turn == 0 else pltpu.roll(by_row[v], turn, 1)
            full = t if full is None else jnp.where(lane16 >= 16 * v, t, full)
        flat[pl.ds(u, 16, stride=4), :] = full.astype(I32)
    to_scalar = pltpu.make_async_copy(flat, sm, sem)
    to_scalar.start()

    lane8 = lax.broadcasted_iota(I32, (8, 128), 1)
    for half in range(2):
        for which in range(2):
            full = None
            for y in range(4):
                tile = gb_ref[pl.ds(pl.multiple_of(16 * (8 * c + 4 * half + y) + 8, 8), 8), :]
                turn = (32 * (y - 2 - which)) % 128
                t = tile if turn == 0 else pltpu.roll(tile, turn, 1)
                full = t if full is None else jnp.where(lane8 >= 32 * y, t, full)
            pq[8 * which : 8 * which + 8, 128 * half : 128 * half + 128] = full.astype(I32)

    left = lane16 < 64

    def assemble(cc, carry):
        for xx in range(4):
            even, odd = 32 * xx + cc, 32 * xx + 16 + cc
            tops = [ga_ref[pl.ds(pl.multiple_of(16 * d, 16), 16), :] for d in (even, odd)]
            lows = [
                jnp.concatenate(
                    [
                        gb_ref[pl.ds(pl.multiple_of(16 * d, 16), 8), :],
                        gc_ref[pl.ds(pl.multiple_of(8 * d, 8), 8), :],
                    ],
                    axis=0,
                )
                for d in (even, odd)
            ]
            for low, (a, b) in enumerate((tops, lows)):
                for which in range(2):
                    if which == 0:
                        full = jnp.where(left, a, pltpu.roll(b, 64, 1))
                    else:
                        full = jnp.where(left, pltpu.roll(a, 64, 1), b)
                    hi = full.astype(BF16)
                    lo = (full - hi.astype(F32)).astype(BF16)
                    at = pl.ds(pl.multiple_of(512 * which + 32 * cc + 16 * low, 16), 16)
                    xh[at, 128 * xx : 128 * xx + 128] = hi
                    xh[at, 512 + 128 * xx : 640 + 128 * xx] = lo
        return carry

    lax.fori_loop(0, 16, assemble, 0)

    place = lax.broadcasted_iota(I32, (512, 256), 0)

    def tables(n, carry):
        which, l = n // 8, n % 8
        picked = pq[pl.ds(n, 1), :]
        hot = jnp.where(place == picked, 1.0, 0.0).astype(BF16)
        t = jnp.dot(
            xh[pl.ds(pl.multiple_of(512 * which, 512), 512), :],
            jnp.concatenate([hot, hot], axis=0),
            preferred_element_type=F32,
        )
        tx[pl.ds(8192 * which + l, 512, stride=16), :] = t[:, 0:128]
        tx[pl.ds(8192 * which + 8 + l, 512, stride=16), :] = t[:, 128:256]
        return carry

    lax.fori_loop(0, 16, tables, 0)
    to_scalar.wait()

    sub = lax.broadcasted_iota(I32, (8, 128), 0)
    low4, low2, low1 = sub < 4, sub % 4 < 2, sub % 2 < 1

    def folded(a):
        b = [
            jnp.where(low4, a[v], a[v + 4]) + pltpu.roll(jnp.where(low4, a[v + 4], a[v]), 4, 0)
            for v in range(4)
        ]
        d = [
            jnp.where(low2, b[v], pltpu.roll(b[v + 2], 2, 0))
            + jnp.where(low2, pltpu.roll(b[v], 6, 0), b[v + 2])
            for v in range(2)
        ]
        return jnp.where(low1, d[0], pltpu.roll(d[1], 1, 0)) + jnp.where(
            low1, pltpu.roll(d[0], 7, 0), d[1]
        )

    def fold_group(n, slot):
        at = pl.ds(pl.multiple_of(8 * n, 8), 8)
        for half in range(2):
            here = [acc[pl.ds(pl.multiple_of(128 * slot + 64 * half + 8 * v, 8), 8), :] for v in range(8)]
            out_ref[at, 128 * half : 128 * half + 128] = folded(here)

    def group(n, carry):
        slot = n % 2
        fold_group(jnp.maximum(n - 1, 0), 1 - slot)
        for v in range(8):
            a0, a1 = None, None
            for k in range(8):
                p = pl.multiple_of(sm[n, 16 * v + k], 8)
                q = pl.multiple_of(sm[n, 16 * v + 8 + k], 8)
                s0 = tx[pl.ds(q, 8), :] * tx[pl.ds(p + 8192, 8), :]
                s1 = tx[pl.ds(q + 8, 8), :] * tx[pl.ds(p + 8200, 8), :]
                a0 = s0 if a0 is None else a0 + s0
                a1 = s1 if a1 is None else a1 + s1
            acc[pl.ds(pl.multiple_of(128 * slot + 8 * v, 8), 8), :] = a0
            acc[pl.ds(pl.multiple_of(128 * slot + 64 + 8 * v, 8), 8), :] = a1
        return carry

    lax.fori_loop(0, 64, group, 0)
    fold_group(63, 1)


def gather(x, w, pos, cnt):
    dma = pltpu.SemaphoreType.DMA
    return pl.pallas_call(
        gather_kernel,
        out_shape=tuple(jax.ShapeDtypeStruct((4, 2, 4, 4, n, 128), F32) for n in (16, 16, 8)),
        in_specs=[pl.BlockSpec(memory_space=pltpu.HBM)] * 4,
        out_specs=tuple(pl.BlockSpec(memory_space=pltpu.VMEM) for n in range(3)),
        scratch_shapes=[
            pltpu.VMEM((31, 62), F32),
            pltpu.VMEM((31, 62), F32),
            pltpu.VMEM((16, 32), I32),
            pltpu.VMEM((32,), I32),
            pltpu.VMEM((16, 128), F32),
            pltpu.VMEM((16, 128), F32),
            pltpu.VMEM((8, 128), F32),
            dma((7,)),
            dma((3,)),
            dma((3,)),
            dma((3,)),
            dma((3,)),
            dma((3,)),
            dma((3, 3)),
            dma((3, 3)),
            dma((3,)),
        ],
        compiler_params=pltpu.CompilerParams(collective_id=0, has_side_effects=True, vmem_limit_bytes=8 << 20),
        name="gather",
    )(x, w, pos, cnt)


def tabled(ga, gb, gc):
    return pl.pallas_call(
        table_kernel,
        out_shape=jax.ShapeDtypeStruct((512, 256), F32),
        in_specs=[pl.BlockSpec(memory_space=pltpu.VMEM)] * 3,
        out_specs=pl.BlockSpec(memory_space=pltpu.VMEM),
        scratch_shapes=[
            pltpu.SMEM((64, 128), I32),
            pltpu.VMEM((64, 128), I32),
            pltpu.VMEM((1024, 1024), BF16),
            pltpu.VMEM((16384, 128), F32),
            pltpu.VMEM((16, 256), I32),
            pltpu.SemaphoreType.DMA,
            pltpu.VMEM((256, 128), F32),
        ],
        compiler_params=pltpu.CompilerParams(vmem_limit_bytes=40 << 20),
        name="tables",
    )(ga, gb, gc)


def shards(moment_x, zinv, positions, entry_count):
    g = gather(*(pltpu.with_memory_space_constraint(a, pltpu.HBM) for a in (moment_x.T, zinv.T, positions.T, entry_count)))
    return tabled(*(a.reshape(-1, 128) for a in g))


def solution(mesh):
    return jax.shard_map(
        shards,
        mesh=mesh,
        in_specs=(P("row", "col"), P("row", "col"), P(("row", "col"), None), P(("row", "col"))),
        out_specs=P("row", "col"),
        check_vma=False,
    )
```

```python
import functools

import jax
import jax.numpy as jnp
from jax import lax
from jax.experimental import pallas as pl
from jax.experimental.pallas import tpu as pltpu
from jax.sharding import PartitionSpec as P

MESH = pl.DeviceIdType.MESH
F32 = jnp.float32
BF16 = jnp.bfloat16
I32 = jnp.int32


def padded(v, part, factor, pad):
    return v + pad * lax.shift_right_logical(v * factor, 16)


def gather_kernel(
    x_in, w_in, pos_in, cnt_in, gi, xh, hot,
    ga, gc, x_ref, w_ref, pos_ref, cnt_ref, slab_a, slab_c, slab_i, pq, loc, s1, s2, s3, sp, r1, r2, r3, rp,
):
    r = lax.axis_index("row")
    c = lax.axis_index("col")
    core = r % 2
    here = (r // 2, c // 4, c % 4)
    ins = [
        pltpu.make_async_copy(a, b, loc.at[n])
        for n, (a, b) in enumerate(((x_in, x_ref), (w_in, w_ref), (pos_in, pos_ref), (cnt_in, cnt_ref)))
    ]
    for copy in ins:
        copy.start()

    def moved(axis, offset):
        at = list(here)
        at[axis] = (at[axis] + offset) % 4
        return at

    def device(at):
        return (2 * at[0] + core, 4 * at[1] + at[2])

    partner = (r + 1 - 2 * core, c)
    barrier = pltpu.get_barrier_semaphore()
    for axis in range(3):
        for offset in (1, 3, 2):
            pl.semaphore_signal(barrier, inc=1, device_id=device(moved(axis, offset)), device_id_type=MESH)
    pl.semaphore_signal(barrier, inc=1, device_id=partner, device_id_type=MESH)

    for ref in (slab_a, slab_c, slab_i):
        ref[...] = jnp.zeros_like(ref)
    for copy in ins:
        copy.wait()
    for lanes, src in ((0, x_ref), (64, w_ref)):
        slab_a[:, lanes : lanes + 62] = src[0:16, :]
        slab_c[0:15, lanes : lanes + 62] = src[16:31, :]

    pos = pos_ref[...]
    live = lax.broadcasted_iota(I32, (16, 32), 0) % 8 < cnt_ref[...].reshape(1, 32)
    cols = jnp.where(live, padded(pos, 62, 1058, 2), 62).astype(F32)
    rows = jnp.where(live, padded(pos, 31, 2115, 1), 31).astype(F32) * 8.0
    rows = jnp.transpose(rows)
    for u in range(4):
        slab_i[:, 16 * u : 16 * u + 16] = rows[8 * u : 8 * u + 8, :]
    slab_i[:, 64:96] = cols[0:8, :]
    slab_i[:, 96:128] = cols[8:16, :]

    every = pl.ds(0, 4)
    parts = ((gi, slab_i, (2, 1, 0)), (ga, slab_a, (2, 0, 1)), (gc, slab_c, (1, 0, 2)))

    def box(g, at, open_axes=()):
        index = [every if axis in open_axes else at[axis] for axis in range(3)]
        return g.at[index[0], core, index[1], index[2]]

    own = [
        pltpu.make_async_copy(slab, box(g, here), loc.at[4 + n]) for n, (g, slab, order) in enumerate(parts)
    ]
    for copy in own:
        copy.start()
    pl.semaphore_wait(barrier, 10)

    def send(src, dst, send_sem, recv_sem, to):
        pltpu.make_async_remote_copy(
            src, dst, send_sem, recv_sem, device_id=to, device_id_type=MESH
        ).start()

    def wait(ref, sem):
        pltpu.make_async_copy(ref, ref, sem).wait()

    for n, (g, slab, order) in enumerate(parts):
        for offset in (1, 3, 2):
            send(slab, box(g, here), s1.at[n], r1.at[n], device(moved(order[0], offset)))
    for copy in own:
        copy.wait()
    for n, (g, slab, order) in enumerate(parts):
        wait(g.at[0, 0, 0, 0:3], r1.at[n])
        line = box(g, here, order[:1])
        for offset in (1, 3, 2):
            send(line, line, s2.at[n], r2.at[n, offset - 1], device(moved(order[1], offset)))
        for offset in (1, 3, 2):
            send(line, line, s3.at[n], r3.at[n, offset - 1], device(moved(order[2], offset)))
    for back in (1, 3, 2):
        for n, (g, slab, order) in enumerate(parts):
            wait(g.at[0, 0, 0, 0:4], r2.at[n, back - 1])
            line = box(g, moved(order[1], 4 - back), order[:1])
            for offset in (1, 3, 2):
                send(line, line, s3.at[n], r3.at[n, offset - 1], device(moved(order[2], offset)))
    left = lax.broadcasted_iota(I32, (16, 128), 1) < 64

    def split(g, plane, along_z, first):
        for step in range(4):
            z, y = (plane, step) if along_z else (step, plane)
            for xx in range(4):
                even, odd = g[xx, 0, z, y], g[xx, 1, z, y]
                both = (
                    jnp.where(left, even, pltpu.roll(odd, 64, 1)),
                    jnp.where(left, pltpu.roll(even, 64, 1), odd),
                )
                for which, full in enumerate(both):
                    hi = full.astype(BF16)
                    lo = (full - hi.astype(F32)).astype(BF16)
                    at = pl.ds(pl.multiple_of(512 * which + 32 * (4 * z + y) + first, 16), 16)
                    xh[at, 128 * xx : 128 * xx + 128] = hi
                    xh[at, 512 + 128 * xx : 640 + 128 * xx] = lo

    def arrived(back):
        for n, (g, slab, order) in enumerate(parts):
            wait(g.at[0, 0], rp.at[n, back])

    def split_both(back):
        split(ga, moved(1, (4 - back) % 4)[1], True, 0)
        split(gc, moved(2, (4 - back) % 4)[2], False, 16)

    for n, (g, slab, order) in enumerate(parts):
        plane = box(g, here, order[:2])
        send(plane, plane, sp.at[n], rp.at[n, 0], partner)
    arrived(0)
    split_both(0)
    for back in (1, 3, 2):
        for n, (g, slab, order) in enumerate(parts):
            wait(g.at[0, 0], r3.at[n, back - 1])
            plane = box(g, moved(order[2], 4 - back), order[:2])
            send(plane, plane, sp.at[n], rp.at[n, back], partner)
    for back in (1, 3):
        arrived(back)
        split_both(back)
    arrived(2)

    lane8 = lax.broadcasted_iota(I32, (8, 128), 1)
    zz, yy = here[1], here[2]
    for half in range(2):
        for which in range(2):
            full = None
            for y in range(4):
                tile = gi[zz, yy // 2, 2 * (yy % 2) + half, y]
                turn = (32 * (y - 2 - which)) % 128
                t = tile if turn == 0 else pltpu.roll(tile, turn, 1)
                full = t if full is None else jnp.where(lane8 >= 32 * y, t, full)
            pq[8 * which : 8 * which + 8, 128 * half : 128 * half + 128] = full.astype(I32)

    place = lax.broadcasted_iota(I32, (512, 256), 0)

    def columns(n, carry):
        hot[n] = jnp.where(place == pq[pl.ds(n, 1), :], 1.0, 0.0).astype(BF16)
        return carry

    lax.fori_loop(0, 16, columns, 0)
    split_both(2)
    for n, (g, slab, order) in enumerate(parts):
        wait(g.at[0, 0, 0, 0:3], s1.at[n])
        wait(g.at[0, 0, 0:3], s2.at[n])
        wait(g.at[0:3, 0], s3.at[n])
        wait(g.at[:, 0], sp.at[n])


def table_kernel(gi_ref, xh, hot, out_ref, sm, flat, tx, acc, rows_out, sem):
    r = lax.axis_index("row")
    lane16 = lax.broadcasted_iota(I32, (16, 128), 1)
    by_row = [gi_ref[pl.ds(128 * r + v, 16, stride=8), :] for v in range(8)]
    for u in range(4):
        full = None
        for v in range(8):
            turn = (16 * (v - u)) % 128
            t = by_row[v] if turn == 0 else pltpu.roll(by_row[v], turn, 1)
            full = t if full is None else jnp.where(lane16 >= 16 * v, t, full)
        flat[pl.ds(u, 16, stride=4), :] = full.astype(I32)
    to_scalar = pltpu.make_async_copy(flat, sm, sem.at[0])
    to_scalar.start()

    def tables(nn, *units):
        for extra in range(2):
            n = 2 * nn + extra
            which, l = n // 8, n % 8
            for unit in range(2):
                sums = units[2 * extra + unit]
                rows = pl.ds(pl.multiple_of(512 * which + 256 * unit, 256), 256)
                for half in range(2):
                    pltpu.matmul_push_rhs(hot[n, 256 * half : 256 * half + 256, :], half, unit)
                for half in range(2):
                    pltpu.matmul_acc_lhs(sums, xh[rows, 256 * half : 256 * half + 256], load_staged_rhs=half)
                    pltpu.matmul_acc_lhs(sums, xh[rows, 512 + 256 * half : 768 + 256 * half])
            for unit in range(2):
                t = pltpu.matmul_pop(units[2 * extra + unit])
                tx[pl.ds(8208 * which + 2048 * unit + l, 256, stride=8), :] = t[:, 0:128]
                tx[pl.ds(8208 * which + 4104 + 2048 * unit + l, 256, stride=8), :] = t[:, 128:256]

    def scoped(nn, carry):
        pl.run_scoped(functools.partial(tables, nn), *(pltpu.ACC(unit)((256, 256), F32) for unit in (0, 1, 0, 1)))
        return carry

    lax.fori_loop(0, 8, scoped, 0)
    to_scalar.wait()

    sub = lax.broadcasted_iota(I32, (8, 128), 0)
    low4, low2, low1 = sub < 4, sub % 4 < 2, sub % 2 < 1

    def folded(a):
        b = [
            jnp.where(low4, a[v], a[v + 4]) + pltpu.roll(jnp.where(low4, a[v + 4], a[v]), 4, 0)
            for v in range(4)
        ]
        d = [
            jnp.where(low2, b[v], pltpu.roll(b[v + 2], 2, 0))
            + jnp.where(low2, pltpu.roll(b[v], 6, 0), b[v + 2])
            for v in range(2)
        ]
        return jnp.where(low1, d[0], pltpu.roll(d[1], 1, 0)) + jnp.where(
            low1, pltpu.roll(d[0], 7, 0), d[1]
        )

    def fold_group(n, slot):
        at = pl.ds(pl.multiple_of(8 * n, 8), 8)
        for half in range(2):
            here = [acc[pl.ds(pl.multiple_of(128 * slot + 64 * half + 8 * v, 8), 8), :] for v in range(8)]
            rows_out[at, 128 * half : 128 * half + 128] = folded(here)

    def group(n, carry):
        slot = n % 2
        fold_group(jnp.maximum(n - 1, 0), 1 - slot)
        for v in range(8):
            a0, a1 = None, None
            for k in range(8):
                p = pl.multiple_of(sm[n, 16 * v + k], 8)
                q = pl.multiple_of(sm[n, 16 * v + 8 + k], 8)
                s0 = tx[pl.ds(q, 8), :] * tx[pl.ds(p + 8208, 8), :]
                s1 = tx[pl.ds(q + 4104, 8), :] * tx[pl.ds(p + 12312, 8), :]
                a0 = s0 if a0 is None else a0 + s0
                a1 = s1 if a1 is None else a1 + s1
            acc[pl.ds(pl.multiple_of(128 * slot + 8 * v, 8), 8), :] = a0
            acc[pl.ds(pl.multiple_of(128 * slot + 64 + 8 * v, 8), 8), :] = a1
        return carry

    outs = []
    for part in range(4):
        lax.fori_loop(16 * part, 16 * part + 16, group, 0)
        first, last = max(128 * part - 8, 0), 128 * part + 120
        if part == 3:
            fold_group(63, 1)
            last = 512
        outs.append(
            pltpu.make_async_copy(rows_out.at[first:last], out_ref.at[first:last], sem.at[1 + part])
        )
        outs[-1].start()
    for copy in outs:
        copy.wait()


def gather(x, w, pos, cnt):
    dma = pltpu.SemaphoreType.DMA
    vmem = pltpu.VMEM
    return pl.pallas_call(
        gather_kernel,
        out_shape=(
            jax.ShapeDtypeStruct((4, 2, 4, 4, 8, 128), F32),
            jax.ShapeDtypeStruct((1024, 1152), BF16),
            jax.ShapeDtypeStruct((16, 512, 256), BF16),
        ),
        in_specs=[pl.BlockSpec(memory_space=pltpu.HBM)] * 4,
        out_specs=tuple(pl.BlockSpec(memory_space=vmem) for n in range(3)),
        scratch_shapes=[
            vmem((4, 2, 4, 4, 16, 128), F32),
            vmem((4, 2, 4, 4, 16, 128), F32),
            vmem((31, 62), F32),
            vmem((31, 62), F32),
            vmem((16, 32), I32),
            vmem((32,), I32),
            vmem((16, 128), F32),
            vmem((16, 128), F32),
            vmem((8, 128), F32),
            vmem((16, 256), I32),
            dma((7,)),
            dma((3,)),
            dma((3,)),
            dma((3,)),
            dma((3,)),
            dma((3,)),
            dma((3, 3)),
            dma((3, 3)),
            dma((3, 4)),
        ],
        compiler_params=pltpu.CompilerParams(collective_id=0, has_side_effects=True, vmem_limit_bytes=16 << 20),
        name="gather",
    )(x, w, pos, cnt)


def tabled(gi, xh, hot):
    return pl.pallas_call(
        table_kernel,
        out_shape=jax.ShapeDtypeStruct((512, 256), F32),
        in_specs=[pl.BlockSpec(memory_space=pltpu.VMEM)] * 3,
        out_specs=pl.BlockSpec(memory_space=pl.ANY),
        scratch_shapes=[
            pltpu.SMEM((64, 128), I32),
            pltpu.VMEM((64, 128), I32),
            pltpu.VMEM((16416, 128), F32),
            pltpu.VMEM((256, 128), F32),
            pltpu.VMEM((512, 256), F32),
            pltpu.SemaphoreType.DMA((5,)),
        ],
        compiler_params=pltpu.CompilerParams(vmem_limit_bytes=40 << 20),
        name="tables",
    )(gi, xh, hot)


def shards(moment_x, zinv, positions, entry_count):
    ins = (moment_x.T, zinv.T, positions.T, entry_count)
    gi, xh, hot = gather(*(pltpu.with_memory_space_constraint(a, pltpu.HBM) for a in ins))
    return tabled(gi.reshape(1024, 128), xh, hot)


def solution(mesh):
    return jax.shard_map(
        shards,
        mesh=mesh,
        in_specs=(P("row", "col"), P("row", "col"), P(("row", "col"), None), P(("row", "col"))),
        out_specs=P("row", "col"),
        check_vma=False,
    )
```

```python
import functools

import jax
import jax.numpy as jnp
from jax import lax
from jax.experimental import pallas as pl
from jax.experimental.pallas import tpu as pltpu
from jax.sharding import PartitionSpec as P

MESH = pl.DeviceIdType.MESH
F32 = jnp.float32
BF16 = jnp.bfloat16
I32 = jnp.int32


def padded(v, part, factor, pad):
    return v + pad * lax.shift_right_logical(v * factor, 16)


def gather_kernel(
    x_in, w_in, pos_in, cnt_in, xh, hot, lists, ids, bounds,
    gi, ga, gc, listed, keys, x_ref, w_ref, pos_ref, cnt_ref, slab_a, slab_c, slab_i, pq, loc, s1, s2, s3, sp, r1, r2, r3, rp,
):
    r = lax.axis_index("row")
    c = lax.axis_index("col")
    core = r % 2
    here = (r // 2, c // 4, c % 4)
    ins = [
        pltpu.make_async_copy(a, b, loc.at[n])
        for n, (a, b) in enumerate(((x_in, x_ref), (w_in, w_ref), (pos_in, pos_ref), (cnt_in, cnt_ref)))
    ]
    for copy in ins:
        copy.start()

    def moved(axis, offset):
        at = list(here)
        at[axis] = (at[axis] + offset) % 4
        return at

    def device(at):
        return (2 * at[0] + core, 4 * at[1] + at[2])

    partner = (r + 1 - 2 * core, c)
    barrier = pltpu.get_barrier_semaphore()
    for axis in range(3):
        for offset in (1, 3, 2):
            pl.semaphore_signal(barrier, inc=1, device_id=device(moved(axis, offset)), device_id_type=MESH)
    pl.semaphore_signal(barrier, inc=1, device_id=partner, device_id_type=MESH)

    for ref in (slab_a, slab_c, slab_i):
        ref[...] = jnp.zeros_like(ref)
    for copy in ins:
        copy.wait()
    for lanes, src in ((0, x_ref), (64, w_ref)):
        slab_a[:, lanes : lanes + 62] = src[0:16, :]
        slab_c[0:15, lanes : lanes + 62] = src[16:31, :]

    pos = pos_ref[...]
    live = lax.broadcasted_iota(I32, (16, 32), 0) % 8 < cnt_ref[...].reshape(1, 32)
    cols = jnp.where(live, padded(pos, 62, 1058, 2), 62).astype(F32)
    rows = jnp.where(live, padded(pos, 31, 2115, 1), 31).astype(F32) * 8.0
    rows = jnp.transpose(rows)
    for u in range(4):
        slab_i[:, 16 * u : 16 * u + 16] = rows[8 * u : 8 * u + 8, :]
    slab_i[:, 64:96] = cols[0:8, :]
    slab_i[:, 96:128] = cols[8:16, :]

    every = pl.ds(0, 4)
    parts = ((gi, slab_i, (2, 1, 0)), (ga, slab_a, (2, 0, 1)), (gc, slab_c, (1, 0, 2)))

    def box(g, at, open_axes=()):
        index = [every if axis in open_axes else at[axis] for axis in range(3)]
        return g.at[index[0], core, index[1], index[2]]

    own = [
        pltpu.make_async_copy(slab, box(g, here), loc.at[4 + n]) for n, (g, slab, order) in enumerate(parts)
    ]
    for copy in own:
        copy.start()
    pl.semaphore_wait(barrier, 10)

    def send(src, dst, send_sem, recv_sem, to):
        pltpu.make_async_remote_copy(
            src, dst, send_sem, recv_sem, device_id=to, device_id_type=MESH
        ).start()

    def wait(ref, sem):
        pltpu.make_async_copy(ref, ref, sem).wait()

    for n, (g, slab, order) in enumerate(parts):
        for offset in (1, 3, 2):
            send(slab, box(g, here), s1.at[n], r1.at[n], device(moved(order[0], offset)))
    for copy in own:
        copy.wait()
    for n, (g, slab, order) in enumerate(parts):
        wait(g.at[0, 0, 0, 0:3], r1.at[n])
        line = box(g, here, order[:1])
        for offset in (1, 3, 2):
            send(line, line, s2.at[n], r2.at[n, offset - 1], device(moved(order[1], offset)))
        for offset in (1, 3, 2):
            send(line, line, s3.at[n], r3.at[n, offset - 1], device(moved(order[2], offset)))
    for back in (1, 3, 2):
        for n, (g, slab, order) in enumerate(parts):
            wait(g.at[0, 0, 0, 0:4], r2.at[n, back - 1])
            line = box(g, moved(order[1], 4 - back), order[:1])
            for offset in (1, 3, 2):
                send(line, line, s3.at[n], r3.at[n, offset - 1], device(moved(order[2], offset)))
    left = lax.broadcasted_iota(I32, (16, 128), 1) < 64

    def split(g, plane, along_z, first):
        for step in range(4):
            z, y = (plane, step) if along_z else (step, plane)
            for xx in range(4):
                even, odd = g[xx, 0, z, y], g[xx, 1, z, y]
                both = (
                    jnp.where(left, even, pltpu.roll(odd, 64, 1)),
                    jnp.where(left, pltpu.roll(even, 64, 1), odd),
                )
                for which, full in enumerate(both):
                    hi = full.astype(BF16)
                    lo = (full - hi.astype(F32)).astype(BF16)
                    at = pl.ds(pl.multiple_of(512 * which + 32 * (4 * z + y) + first, 16), 16)
                    xh[at, 128 * xx : 128 * xx + 128] = hi
                    xh[at, 512 + 128 * xx : 640 + 128 * xx] = lo

    def sort_rows():
        lane = lax.broadcasted_iota(I32, (8, 128), 1)
        sub = lax.broadcasted_iota(I32, (8, 128), 0)

        def take(m, carry):
            tile = gi[here[0], core, m // 4, m % 4]
            for u in range(4):
                t = tile if u == 0 else pltpu.roll(tile, 128 - 16 * u, 1)
                row = 32 * m + 8 * u + sub
                live = jnp.where((lane >= 8) & (lane < 16) & (t != 248.0), 1.0, 0.0)
                count = jnp.sum(live, axis=1, keepdims=True)
                e = t * 0.125
                h = jnp.floor(e * 0.5)
                low = pltpu.roll(e - 2.0 * h, 16, 1)
                value = jnp.where(lane < 16, h, jnp.where(lane < 32, low, 0.0))
                value = jnp.where(lane == 32, lax.shift_right_logical(row, 1).astype(F32), value)
                value = jnp.where(lane == 33, (row & 1).astype(F32), value)
                value = jnp.where(lane == 34, count, value)
                at = pl.ds(pl.multiple_of(32 * m + 8 * u, 8), 8)
                listed[at, :] = value
                keys[at, :] = count * 512.0 + (511 - row).astype(F32)
            return carry

        lax.fori_loop(0, 16, take, 0)
        key_row = jnp.transpose(keys[...])[0:1, :]

        def above(b, total):
            key = keys[pl.ds(pl.multiple_of(8 * b, 8), 8), :]
            key = jnp.concatenate([key, key, key, key], axis=1)
            return total + jnp.where(key > key_row, 1.0, 0.0)

        total = lax.fori_loop(0, 64, above, jnp.zeros((8, 512), F32))
        place = jnp.sum(total, axis=0, keepdims=True).astype(I32)
        chosen = jnp.where(lax.broadcasted_iota(I32, (512, 512), 0) == place, 1.0, 0.0).astype(BF16)
        keys[...] = jnp.dot(chosen, listed[...].astype(BF16), preferred_element_type=F32)

        lane64 = lax.broadcasted_iota(I32, (64, 128), 1)
        flat, names = None, None
        for v in range(8):
            t = keys[pl.ds(v, 64, stride=8), :]
            slots = 16.0 * t + 8.0 * pltpu.roll(t, 112, 1)
            name = 2.0 * t + pltpu.roll(t, 127, 1)
            if v == 0:
                flat = slots
                names = pltpu.roll(name, 96, 1)
                reach = jnp.where(t[:, 34:35] >= lane64.astype(F32), 1.0, 0.0)
                bounds[...] = jnp.broadcast_to(jnp.sum(reach, axis=0, keepdims=True), (8, 128)).astype(I32)
            else:
                flat = jnp.where(lane64 >= 16 * v, pltpu.roll(slots, 16 * v, 1), flat)
                names = jnp.where(lane64 >= v, pltpu.roll(name, 96 + v, 1), names)
        lists[...] = flat.astype(I32)
        ids[...] = names.astype(I32)

    def arrived(back):
        for n, (g, slab, order) in enumerate(parts):
            wait(g.at[0, 0], rp.at[n, back])

    def split_both(back):
        split(ga, moved(1, (4 - back) % 4)[1], True, 0)
        split(gc, moved(2, (4 - back) % 4)[2], False, 16)

    for n, (g, slab, order) in enumerate(parts):
        plane = box(g, here, order[:2])
        send(plane, plane, sp.at[n], rp.at[n, 0], partner)
    sort_rows()
    arrived(0)
    split_both(0)
    for back in (1, 3, 2):
        for n, (g, slab, order) in enumerate(parts):
            wait(g.at[0, 0], r3.at[n, back - 1])
            plane = box(g, moved(order[2], 4 - back), order[:2])
            send(plane, plane, sp.at[n], rp.at[n, back], partner)
    for back in (1, 3):
        arrived(back)
        split_both(back)
    arrived(2)

    lane8 = lax.broadcasted_iota(I32, (8, 128), 1)
    zz, yy = here[1], here[2]
    for half in range(2):
        for which in range(2):
            full = None
            for y in range(4):
                tile = gi[zz, yy // 2, 2 * (yy % 2) + half, y]
                turn = (32 * (y - 2 - which)) % 128
                t = tile if turn == 0 else pltpu.roll(tile, turn, 1)
                full = t if full is None else jnp.where(lane8 >= 32 * y, t, full)
            pq[8 * which : 8 * which + 8, 128 * half : 128 * half + 128] = full.astype(I32)

    place = lax.broadcasted_iota(I32, (512, 256), 0)

    def columns(n, carry):
        hot[n] = jnp.where(place == pq[pl.ds(n, 1), :], 1.0, 0.0).astype(BF16)
        return carry

    lax.fori_loop(0, 16, columns, 0)
    split_both(2)
    for n, (g, slab, order) in enumerate(parts):
        wait(g.at[0, 0, 0, 0:3], s1.at[n])
        wait(g.at[0, 0, 0:3], s2.at[n])
        wait(g.at[0:3, 0], s3.at[n])
        wait(g.at[:, 0], sp.at[n])


def table_kernel(xh, hot, lists, ids, bounds, out_ref, sm, names, ends, tx, acc, rows_out, sem):
    to_scalar = [
        pltpu.make_async_copy(a, b, sem.at[n])
        for n, (a, b) in enumerate(((lists, sm), (ids, names), (bounds, ends)))
    ]
    for copy in to_scalar:
        copy.start()

    def tables(nn, *units):
        for extra in range(2):
            n = 2 * nn + extra
            which, l = n // 8, n % 8
            for unit in range(2):
                sums = units[2 * extra + unit]
                rows = pl.ds(pl.multiple_of(512 * which + 256 * unit, 256), 256)
                for half in range(2):
                    pltpu.matmul_push_rhs(hot[n, 256 * half : 256 * half + 256, :], half, unit)
                for half in range(2):
                    pltpu.matmul_acc_lhs(sums, xh[rows, 256 * half : 256 * half + 256], load_staged_rhs=half)
                    pltpu.matmul_acc_lhs(sums, xh[rows, 512 + 256 * half : 768 + 256 * half])
            for unit in range(2):
                t = pltpu.matmul_pop(units[2 * extra + unit])
                tx[pl.ds(8208 * which + 2048 * unit + l, 256, stride=8), :] = t[:, 0:128]
                tx[pl.ds(8208 * which + 4104 + 2048 * unit + l, 256, stride=8), :] = t[:, 128:256]

    def scoped(nn, carry):
        pl.run_scoped(functools.partial(tables, nn), *(pltpu.ACC(unit)((256, 256), F32) for unit in (0, 1, 0, 1)))
        return carry

    lax.fori_loop(0, 8, scoped, 0)
    for copy in to_scalar:
        copy.wait()

    sub = lax.broadcasted_iota(I32, (8, 128), 0)
    low4, low2, low1 = sub < 4, sub % 4 < 2, sub % 2 < 1

    def folded(a):
        b = [
            jnp.where(low4, a[v], a[v + 4]) + pltpu.roll(jnp.where(low4, a[v + 4], a[v]), 4, 0)
            for v in range(4)
        ]
        d = [
            jnp.where(low2, b[v], pltpu.roll(b[v + 2], 2, 0))
            + jnp.where(low2, pltpu.roll(b[v], 6, 0), b[v + 2])
            for v in range(2)
        ]
        return jnp.where(low1, d[0], pltpu.roll(d[1], 1, 0)) + jnp.where(
            low1, pltpu.roll(d[0], 7, 0), d[1]
        )

    def fold_group(n, slot):
        for half in range(2):
            here = [acc[pl.ds(pl.multiple_of(128 * slot + 64 * half + 8 * v, 8), 8), :] for v in range(8)]
            sums = folded(here)
            for v in range(8):
                rows_out[pl.ds(512 * half + names[n, v], 1), :] = sums[v : v + 1, :]

    def group(count, n, carry):
        slot = n % 2
        fold_group(jnp.maximum(n - 1, 0), 1 - slot)
        for v in range(8):
            a0, a1 = None, None
            for k in range(count):
                p = pl.multiple_of(sm[n, 16 * v + k], 8)
                q = pl.multiple_of(sm[n, 16 * v + 8 + k], 8)
                s0 = tx[pl.ds(q, 8), :] * tx[pl.ds(p + 8208, 8), :]
                s1 = tx[pl.ds(q + 4104, 8), :] * tx[pl.ds(p + 12312, 8), :]
                a0 = s0 if a0 is None else a0 + s0
                a1 = s1 if a1 is None else a1 + s1
            acc[pl.ds(pl.multiple_of(128 * slot + 8 * v, 8), 8), :] = a0
            acc[pl.ds(pl.multiple_of(128 * slot + 64 + 8 * v, 8), 8), :] = a1
        return carry

    first = jnp.int32(0)
    for count in range(8, 0, -1):
        last = ends[0, count] if count > 1 else jnp.int32(64)
        lax.fori_loop(first, last, functools.partial(group, count), 0)
        first = last
    fold_group(63, 1)
    halves = [
        pltpu.make_async_copy(
            rows_out.at[512 * half : 512 * half + 512], out_ref.at[:, 128 * half : 128 * half + 128], sem.at[half]
        )
        for half in range(2)
    ]
    for copy in halves:
        copy.start()
    for copy in halves:
        copy.wait()


def gather(x, w, pos, cnt):
    dma = pltpu.SemaphoreType.DMA
    vmem = pltpu.VMEM
    return pl.pallas_call(
        gather_kernel,
        out_shape=(
            jax.ShapeDtypeStruct((1024, 1152), BF16),
            jax.ShapeDtypeStruct((16, 512, 256), BF16),
            jax.ShapeDtypeStruct((64, 128), I32),
            jax.ShapeDtypeStruct((64, 128), I32),
            jax.ShapeDtypeStruct((8, 128), I32),
        ),
        in_specs=[pl.BlockSpec(memory_space=pltpu.HBM)] * 4,
        out_specs=tuple(pl.BlockSpec(memory_space=vmem) for n in range(5)),
        scratch_shapes=[
            vmem((4, 2, 4, 4, 8, 128), F32),
            vmem((4, 2, 4, 4, 16, 128), F32),
            vmem((4, 2, 4, 4, 16, 128), F32),
            vmem((512, 128), F32),
            vmem((512, 128), F32),
            vmem((31, 62), F32),
            vmem((31, 62), F32),
            vmem((16, 32), I32),
            vmem((32,), I32),
            vmem((16, 128), F32),
            vmem((16, 128), F32),
            vmem((8, 128), F32),
            vmem((16, 256), I32),
            dma((7,)),
            dma((3,)),
            dma((3,)),
            dma((3,)),
            dma((3,)),
            dma((3,)),
            dma((3, 3)),
            dma((3, 3)),
            dma((3, 4)),
        ],
        compiler_params=pltpu.CompilerParams(collective_id=0, has_side_effects=True, vmem_limit_bytes=16 << 20),
        name="gather",
    )(x, w, pos, cnt)


def tabled(*gathered):
    return pl.pallas_call(
        table_kernel,
        out_shape=jax.ShapeDtypeStruct((512, 256), F32),
        in_specs=[pl.BlockSpec(memory_space=pltpu.VMEM)] * 5,
        out_specs=pl.BlockSpec(memory_space=pl.ANY),
        scratch_shapes=[
            pltpu.SMEM((64, 128), I32),
            pltpu.SMEM((64, 128), I32),
            pltpu.SMEM((8, 128), I32),
            pltpu.VMEM((16416, 128), F32),
            pltpu.VMEM((256, 128), F32),
            pltpu.VMEM((1024, 128), F32),
            pltpu.SemaphoreType.DMA((3,)),
        ],
        compiler_params=pltpu.CompilerParams(vmem_limit_bytes=40 << 20),
        name="tables",
    )(*gathered)


def shards(moment_x, zinv, positions, entry_count):
    ins = (moment_x.T, zinv.T, positions.T, entry_count)
    return tabled(*gather(*(pltpu.with_memory_space_constraint(a, pltpu.HBM) for a in ins)))


def solution(mesh):
    return jax.shard_map(
        shards,
        mesh=mesh,
        in_specs=(P("row", "col"), P("row", "col"), P(("row", "col"), None), P(("row", "col"))),
        out_specs=P("row", "col"),
        check_vma=False,
    )
```

```python
import functools

import jax
import jax.numpy as jnp
from jax import lax
from jax.experimental import pallas as pl
from jax.experimental.pallas import tpu as pltpu
from jax.sharding import PartitionSpec as P

MESH = pl.DeviceIdType.MESH
F32 = jnp.float32
BF16 = jnp.bfloat16
I32 = jnp.int32


def padded(v, part, factor, pad):
    return v + pad * lax.shift_right_logical(v * factor, 16)


def gather_kernel(
    x_in, w_in, pos_in, cnt_in, xh, hot, lists, ids, bounds,
    gi, ga, gc, listed, keys, x_ref, w_ref, pos_ref, cnt_ref, slab_a, slab_c, slab_i, pq, loc, s1, s2, s3, sp, r1, r2, r3, rp,
):
    r = lax.axis_index("row")
    c = lax.axis_index("col")
    core = r % 2
    here = (r // 2, c // 4, c % 4)
    ins = [
        pltpu.make_async_copy(a, b, loc.at[n])
        for n, (a, b) in enumerate(((x_in, x_ref), (w_in, w_ref), (pos_in, pos_ref), (cnt_in, cnt_ref)))
    ]
    for copy in ins:
        copy.start()

    def moved(axis, offset):
        at = list(here)
        at[axis] = (at[axis] + offset) % 4
        return at

    def device(at):
        return (2 * at[0] + core, 4 * at[1] + at[2])

    partner = (r + 1 - 2 * core, c)
    barrier = pltpu.get_barrier_semaphore()
    for axis in range(3):
        for offset in (1, 3, 2):
            pl.semaphore_signal(barrier, inc=1, device_id=device(moved(axis, offset)), device_id_type=MESH)
    pl.semaphore_signal(barrier, inc=1, device_id=partner, device_id_type=MESH)

    for ref in (slab_a, slab_c, slab_i):
        ref[...] = jnp.zeros_like(ref)
    for copy in ins:
        copy.wait()
    for lanes, src in ((0, x_ref), (64, w_ref)):
        slab_a[:, lanes : lanes + 62] = src[0:16, :]
        slab_c[0:15, lanes : lanes + 62] = src[16:31, :]

    pos = pos_ref[...]
    live = lax.broadcasted_iota(I32, (16, 32), 0) % 8 < cnt_ref[...].reshape(1, 32)
    cols = jnp.where(live, padded(pos, 62, 1058, 2), 62).astype(F32)
    rows = jnp.where(live, padded(pos, 31, 2115, 1), 31).astype(F32) * 8.0
    rows = jnp.transpose(rows)
    for u in range(4):
        slab_i[:, 16 * u : 16 * u + 16] = rows[8 * u : 8 * u + 8, :]
    slab_i[:, 64:96] = cols[0:8, :]
    slab_i[:, 96:128] = cols[8:16, :]

    every = pl.ds(0, 4)
    parts = ((gi, slab_i, (2, 1, 0)), (ga, slab_a, (2, 0, 1)), (gc, slab_c, (1, 0, 2)))

    def box(g, at, open_axes=()):
        index = [every if axis in open_axes else at[axis] for axis in range(3)]
        return g.at[index[0], core, index[1], index[2]]

    own = [
        pltpu.make_async_copy(slab, box(g, here), loc.at[4 + n]) for n, (g, slab, order) in enumerate(parts)
    ]
    for copy in own:
        copy.start()
    pl.semaphore_wait(barrier, 10)

    def send(src, dst, send_sem, recv_sem, to):
        pltpu.make_async_remote_copy(
            src, dst, send_sem, recv_sem, device_id=to, device_id_type=MESH
        ).start()

    def wait(ref, sem):
        pltpu.make_async_copy(ref, ref, sem).wait()

    for n, (g, slab, order) in enumerate(parts):
        for offset in (1, 3, 2):
            send(slab, box(g, here), s1.at[n], r1.at[n], device(moved(order[0], offset)))
    for copy in own:
        copy.wait()
    for n, (g, slab, order) in enumerate(parts):
        wait(g.at[0, 0, 0, 0:3], r1.at[n])
        line = box(g, here, order[:1])
        for offset in (1, 3, 2):
            send(line, line, s2.at[n], r2.at[n, offset - 1], device(moved(order[1], offset)))
        for offset in (1, 3, 2):
            send(line, line, s3.at[n], r3.at[n, offset - 1], device(moved(order[2], offset)))
    for back in (1, 3, 2):
        for n, (g, slab, order) in enumerate(parts):
            wait(g.at[0, 0, 0, 0:4], r2.at[n, back - 1])
            line = box(g, moved(order[1], 4 - back), order[:1])
            for offset in (1, 3, 2):
                send(line, line, s3.at[n], r3.at[n, offset - 1], device(moved(order[2], offset)))
    left = lax.broadcasted_iota(I32, (16, 128), 1) < 64

    def split(g, plane, along_z, first):
        for step in range(4):
            z, y = (plane, step) if along_z else (step, plane)
            for xx in range(4):
                even, odd = g[xx, 0, z, y], g[xx, 1, z, y]
                both = (
                    jnp.where(left, even, pltpu.roll(odd, 64, 1)),
                    jnp.where(left, pltpu.roll(even, 64, 1), odd),
                )
                for which, full in enumerate(both):
                    hi = full.astype(BF16)
                    lo = (full - hi.astype(F32)).astype(BF16)
                    at = pl.ds(pl.multiple_of(512 * which + 32 * (4 * z + y) + first, 16), 16)
                    xh[at, 128 * xx : 128 * xx + 128] = hi
                    xh[at, 512 + 128 * xx : 640 + 128 * xx] = lo

    def sort_rows():
        lane = lax.broadcasted_iota(I32, (8, 128), 1)
        sub = lax.broadcasted_iota(I32, (8, 128), 0)

        def take(m, carry):
            tile = gi[here[0], core, m // 4, m % 4]
            for u in range(4):
                t = tile if u == 0 else pltpu.roll(tile, 128 - 16 * u, 1)
                row = 32 * m + 8 * u + sub
                live = jnp.where((lane >= 8) & (lane < 16) & (t != 248.0), 1.0, 0.0)
                count = jnp.sum(live, axis=1, keepdims=True)
                e = t * 0.125
                h = jnp.floor(e * 0.5)
                low = pltpu.roll(e - 2.0 * h, 16, 1)
                value = jnp.where(lane < 16, h, jnp.where(lane < 32, low, 0.0))
                value = jnp.where(lane == 32, lax.shift_right_logical(row, 1).astype(F32), value)
                value = jnp.where(lane == 33, (row & 1).astype(F32), value)
                value = jnp.where(lane == 34, count, value)
                at = pl.ds(pl.multiple_of(32 * m + 8 * u, 8), 8)
                listed[at, :] = value
                keys[at, :] = count * 512.0 + (511 - row).astype(F32)
            return carry

        lax.fori_loop(0, 16, take, 0)
        key_row = jnp.transpose(keys[...])[0:1, :]

        def above(b, total):
            key = keys[pl.ds(pl.multiple_of(8 * b, 8), 8), :]
            key = jnp.concatenate([key, key, key, key], axis=1)
            return total + jnp.where(key > key_row, 1.0, 0.0)

        total = lax.fori_loop(0, 64, above, jnp.zeros((8, 512), F32))
        place = jnp.sum(total, axis=0, keepdims=True).astype(I32)
        chosen = jnp.where(lax.broadcasted_iota(I32, (512, 512), 0) == place, 1.0, 0.0).astype(BF16)
        keys[...] = jnp.dot(chosen, listed[...].astype(BF16), preferred_element_type=F32)

        lane64 = lax.broadcasted_iota(I32, (64, 128), 1)
        flat, names = None, None
        for v in range(8):
            t = keys[pl.ds(v, 64, stride=8), :]
            slots = 16.0 * t + 8.0 * pltpu.roll(t, 112, 1)
            name = 2.0 * t + pltpu.roll(t, 127, 1)
            if v == 0:
                flat = slots
                names = pltpu.roll(name, 96, 1)
                reach = jnp.where(t[:, 34:35] >= lane64.astype(F32), 1.0, 0.0)
                bounds[...] = jnp.broadcast_to(jnp.sum(reach, axis=0, keepdims=True), (8, 128)).astype(I32)
            else:
                flat = jnp.where(lane64 >= 16 * v, pltpu.roll(slots, 16 * v, 1), flat)
                names = jnp.where(lane64 >= v, pltpu.roll(name, 96 + v, 1), names)
        lists[...] = flat.astype(I32)
        ids[...] = names.astype(I32)

    def arrived(back, start):
        for n in range(start, 3):
            wait(parts[n][0].at[0, 0], rp.at[n, back])

    def split_both(back):
        split(ga, moved(1, (4 - back) % 4)[1], True, 0)
        split(gc, moved(2, (4 - back) % 4)[2], False, 16)

    for n, (g, slab, order) in enumerate(parts):
        plane = box(g, here, order[:2])
        send(plane, plane, sp.at[n], rp.at[n, 0], partner)
    sort_rows()
    arrived(0, 0)
    split_both(0)
    for back in (1, 3, 2):
        for n, (g, slab, order) in enumerate(parts):
            wait(g.at[0, 0], r3.at[n, back - 1])
            plane = box(g, moved(order[2], 4 - back), order[:2])
            send(plane, plane, sp.at[n], rp.at[n, back], partner)
    for back in (1, 3):
        arrived(back, 1)
        split_both(back)
    for back in (1, 3, 2):
        wait(gi.at[0, 0], rp.at[0, back])

    lane8 = lax.broadcasted_iota(I32, (8, 128), 1)
    zz, yy = here[1], here[2]
    for half in range(2):
        for which in range(2):
            full = None
            for y in range(4):
                tile = gi[zz, yy // 2, 2 * (yy % 2) + half, y]
                turn = (32 * (y - 2 - which)) % 128
                t = tile if turn == 0 else pltpu.roll(tile, turn, 1)
                full = t if full is None else jnp.where(lane8 >= 32 * y, t, full)
            pq[8 * which : 8 * which + 8, 128 * half : 128 * half + 128] = full.astype(I32)

    place = lax.broadcasted_iota(I32, (512, 256), 0)

    def columns(n, carry):
        hot[n] = jnp.where(place == pq[pl.ds(n, 1), :], 1.0, 0.0).astype(BF16)
        return carry

    lax.fori_loop(0, 16, columns, 0)
    arrived(2, 1)
    split_both(2)
    for n, (g, slab, order) in enumerate(parts):
        wait(g.at[0, 0, 0, 0:3], s1.at[n])
        wait(g.at[0, 0, 0:3], s2.at[n])
        wait(g.at[0:3, 0], s3.at[n])
        wait(g.at[:, 0], sp.at[n])


def table_kernel(xh, hot, lists, ids, bounds, out_ref, sm, names, ends, tx, acc, rows_out, sem):
    to_scalar = [
        pltpu.make_async_copy(a, b, sem.at[n])
        for n, (a, b) in enumerate(((lists, sm), (ids, names), (bounds, ends)))
    ]
    for copy in to_scalar:
        copy.start()

    def tables(nn, *units):
        for extra in range(2):
            n = 2 * nn + extra
            which, l = n // 8, n % 8
            for unit in range(2):
                sums = units[2 * extra + unit]
                rows = pl.ds(pl.multiple_of(512 * which + 256 * unit, 256), 256)
                for half in range(2):
                    pltpu.matmul_push_rhs(hot[n, 256 * half : 256 * half + 256, :], half, unit)
                for half in range(2):
                    pltpu.matmul_acc_lhs(sums, xh[rows, 256 * half : 256 * half + 256], load_staged_rhs=half)
                    pltpu.matmul_acc_lhs(sums, xh[rows, 512 + 256 * half : 768 + 256 * half])
            for unit in range(2):
                t = pltpu.matmul_pop(units[2 * extra + unit])
                tx[pl.ds(8208 * which + 2048 * unit + l, 256, stride=8), :] = t[:, 0:128]
                tx[pl.ds(8208 * which + 4104 + 2048 * unit + l, 256, stride=8), :] = t[:, 128:256]

    def scoped(nn, carry):
        pl.run_scoped(functools.partial(tables, nn), *(pltpu.ACC(unit)((256, 256), F32) for unit in (0, 1, 0, 1)))
        return carry

    lax.fori_loop(0, 8, scoped, 0)
    for copy in to_scalar:
        copy.wait()

    sub = lax.broadcasted_iota(I32, (8, 128), 0)
    low4, low2, low1 = sub < 4, sub % 4 < 2, sub % 2 < 1

    def folded(a):
        b = [
            jnp.where(low4, a[v], a[v + 4]) + pltpu.roll(jnp.where(low4, a[v + 4], a[v]), 4, 0)
            for v in range(4)
        ]
        d = [
            jnp.where(low2, b[v], pltpu.roll(b[v + 2], 2, 0))
            + jnp.where(low2, pltpu.roll(b[v], 6, 0), b[v + 2])
            for v in range(2)
        ]
        return jnp.where(low1, d[0], pltpu.roll(d[1], 1, 0)) + jnp.where(
            low1, pltpu.roll(d[0], 7, 0), d[1]
        )

    def fold_group(n, slot):
        for half in range(2):
            here = [acc[pl.ds(pl.multiple_of(128 * slot + 64 * half + 8 * v, 8), 8), :] for v in range(8)]
            sums = folded(here)
            for v in range(8):
                rows_out[pl.ds(512 * half + names[n, v], 1), :] = sums[v : v + 1, :]

    def group(count, n, carry):
        slot = n % 2
        fold_group(jnp.maximum(n - 1, 0), 1 - slot)
        for v in range(8):
            a0, a1 = None, None
            for k in range(count):
                p = pl.multiple_of(sm[n, 16 * v + k], 8)
                q = pl.multiple_of(sm[n, 16 * v + 8 + k], 8)
                s0 = tx[pl.ds(q, 8), :] * tx[pl.ds(p + 8208, 8), :]
                s1 = tx[pl.ds(q + 4104, 8), :] * tx[pl.ds(p + 12312, 8), :]
                a0 = s0 if a0 is None else a0 + s0
                a1 = s1 if a1 is None else a1 + s1
            acc[pl.ds(pl.multiple_of(128 * slot + 8 * v, 8), 8), :] = a0
            acc[pl.ds(pl.multiple_of(128 * slot + 64 + 8 * v, 8), 8), :] = a1
        return carry

    first = jnp.int32(0)
    for count in range(8, 0, -1):
        last = ends[0, count] if count > 1 else jnp.int32(64)
        lax.fori_loop(first, last, functools.partial(group, count), 0)
        first = last
    fold_group(63, 1)
    halves = [
        pltpu.make_async_copy(
            rows_out.at[512 * half : 512 * half + 512], out_ref.at[:, 128 * half : 128 * half + 128], sem.at[half]
        )
        for half in range(2)
    ]
    for copy in halves:
        copy.start()
    for copy in halves:
        copy.wait()


def gather(x, w, pos, cnt):
    dma = pltpu.SemaphoreType.DMA
    vmem = pltpu.VMEM
    return pl.pallas_call(
        gather_kernel,
        out_shape=(
            jax.ShapeDtypeStruct((1024, 1152), BF16),
            jax.ShapeDtypeStruct((16, 512, 256), BF16),
            jax.ShapeDtypeStruct((64, 128), I32),
            jax.ShapeDtypeStruct((64, 128), I32),
            jax.ShapeDtypeStruct((8, 128), I32),
        ),
        in_specs=[pl.BlockSpec(memory_space=pltpu.HBM)] * 4,
        out_specs=tuple(pl.BlockSpec(memory_space=vmem) for n in range(5)),
        scratch_shapes=[
            vmem((4, 2, 4, 4, 8, 128), F32),
            vmem((4, 2, 4, 4, 16, 128), F32),
            vmem((4, 2, 4, 4, 16, 128), F32),
            vmem((512, 128), F32),
            vmem((512, 128), F32),
            vmem((31, 62), F32),
            vmem((31, 62), F32),
            vmem((16, 32), I32),
            vmem((32,), I32),
            vmem((16, 128), F32),
            vmem((16, 128), F32),
            vmem((8, 128), F32),
            vmem((16, 256), I32),
            dma((7,)),
            dma((3,)),
            dma((3,)),
            dma((3,)),
            dma((3,)),
            dma((3,)),
            dma((3, 3)),
            dma((3, 3)),
            dma((3, 4)),
        ],
        compiler_params=pltpu.CompilerParams(collective_id=0, has_side_effects=True, vmem_limit_bytes=16 << 20),
        name="gather",
    )(x, w, pos, cnt)


def tabled(*gathered):
    return pl.pallas_call(
        table_kernel,
        out_shape=jax.ShapeDtypeStruct((512, 256), F32),
        in_specs=[pl.BlockSpec(memory_space=pltpu.VMEM)] * 5,
        out_specs=pl.BlockSpec(memory_space=pl.ANY),
        scratch_shapes=[
            pltpu.SMEM((64, 128), I32),
            pltpu.SMEM((64, 128), I32),
            pltpu.SMEM((8, 128), I32),
            pltpu.VMEM((16416, 128), F32),
            pltpu.VMEM((256, 128), F32),
            pltpu.VMEM((1024, 128), F32),
            pltpu.SemaphoreType.DMA((3,)),
        ],
        compiler_params=pltpu.CompilerParams(vmem_limit_bytes=40 << 20),
        name="tables",
    )(*gathered)


def shards(moment_x, zinv, positions, entry_count):
    ins = (moment_x.T, zinv.T, positions.T, entry_count)
    return tabled(*gather(*(pltpu.with_memory_space_constraint(a, pltpu.HBM) for a in ins)))


def solution(mesh):
    return jax.shard_map(
        shards,
        mesh=mesh,
        in_specs=(P("row", "col"), P("row", "col"), P(("row", "col"), None), P(("row", "col"))),
        out_specs=P("row", "col"),
        check_vma=False,
    )
```

```python
import functools

import jax
import jax.numpy as jnp
from jax import lax
from jax.experimental import pallas as pl
from jax.experimental.pallas import tpu as pltpu
from jax.sharding import PartitionSpec as P

MESH = pl.DeviceIdType.MESH
F32 = jnp.float32
BF16 = jnp.bfloat16
I32 = jnp.int32


def padded(v, part, factor, pad):
    return v + pad * lax.shift_right_logical(v * factor, 16)


def gather_kernel(
    x_in, w_in, pos_in, cnt_in, xh, hot, lists, ids, bounds,
    gi, ga, gc, listed, keys, x_ref, w_ref, pos_ref, cnt_ref, slab_a, slab_c, slab_i, pq, loc, s1, s3, sp, r1, r3, rp,
):
    r = lax.axis_index("row")
    c = lax.axis_index("col")
    core = r % 2
    here = (r // 2, c // 4, c % 4)
    ins = [
        pltpu.make_async_copy(a, b, loc.at[n])
        for n, (a, b) in enumerate(((x_in, x_ref), (w_in, w_ref), (pos_in, pos_ref), (cnt_in, cnt_ref)))
    ]
    for copy in ins:
        copy.start()

    def moved(axis, offset):
        at = list(here)
        at[axis] = (at[axis] + offset) % 4
        return at

    def device(at):
        return (2 * at[0] + core, 4 * at[1] + at[2])

    partner = (r + 1 - 2 * core, c)
    barrier = pltpu.get_barrier_semaphore()
    near = [
        (dx, dz, dy)
        for dx in range(4)
        for dz in range(4)
        for dy in range(4)
        if dx * dz * dy == 0 and dx + dz + dy > 0
    ]
    near.sort(key=lambda o: -sum(min(v, 4 - v) for v in o))

    def shifted(offsets):
        return [(at + o) % 4 if o else at for at, o in zip(here, offsets)]

    for offsets in near:
        pl.semaphore_signal(barrier, inc=1, device_id=device(shifted(offsets)), device_id_type=MESH)
    pl.semaphore_signal(barrier, inc=1, device_id=partner, device_id_type=MESH)

    for ref in (slab_a, slab_c, slab_i):
        ref[...] = jnp.zeros_like(ref)
    for copy in ins:
        copy.wait()
    for lanes, src in ((0, x_ref), (64, w_ref)):
        slab_a[:, lanes : lanes + 62] = src[0:16, :]
        slab_c[0:15, lanes : lanes + 62] = src[16:31, :]

    pos = pos_ref[...]
    live = lax.broadcasted_iota(I32, (16, 32), 0) % 8 < cnt_ref[...].reshape(1, 32)
    cols = jnp.where(live, padded(pos, 62, 1058, 2), 62).astype(F32)
    rows = jnp.where(live, padded(pos, 31, 2115, 1), 31).astype(F32) * 8.0
    rows = jnp.transpose(rows)
    for u in range(4):
        slab_i[:, 16 * u : 16 * u + 16] = rows[8 * u : 8 * u + 8, :]
    slab_i[:, 64:96] = cols[0:8, :]
    slab_i[:, 96:128] = cols[8:16, :]

    every = pl.ds(0, 4)
    parts = ((gi, slab_i, (2, 1, 0)), (ga, slab_a, (2, 0, 1)), (gc, slab_c, (1, 0, 2)))

    def box(g, at, open_axes=()):
        index = [every if axis in open_axes else at[axis] for axis in range(3)]
        return g.at[index[0], core, index[1], index[2]]

    own = [
        pltpu.make_async_copy(slab, box(g, here), loc.at[4 + n]) for n, (g, slab, order) in enumerate(parts)
    ]
    for copy in own:
        copy.start()
    pl.semaphore_wait(barrier, len(near) + 1)

    def send(src, dst, send_sem, recv_sem, to):
        pltpu.make_async_remote_copy(
            src, dst, send_sem, recv_sem, device_id=to, device_id_type=MESH
        ).start()

    def wait(ref, sem):
        pltpu.make_async_copy(ref, ref, sem).wait()

    for step in (0, 1, 3, 2):
        for side in (2, 1, 3, 0):
            for n, (g, slab, order) in enumerate(parts):
                if step or side:
                    offsets = [0, 0, 0]
                    offsets[order[0]], offsets[order[1]] = step, side
                    send(slab, box(g, here), s1.at[n, min(step, 1)], r1.at[n, step], device(shifted(offsets)))
    for copy in own:
        copy.wait()
    for back in (0, 1, 3, 2):
        for n, (g, slab, order) in enumerate(parts):
            wait(g.at[0, 0, 0, 0 : 4 if back else 3], r1.at[n, back])
            line = box(g, moved(order[0], (4 - back) % 4), order[1:2])
            for offset in (1, 3, 2):
                send(line, line, s3.at[n], r3.at[n, offset - 1], device(moved(order[2], offset)))
    left = lax.broadcasted_iota(I32, (16, 128), 1) < 64

    def split(g, plane, along_z, first):
        for step in range(4):
            z, y = (plane, step) if along_z else (step, plane)
            for xx in range(4):
                even, odd = g[xx, 0, z, y], g[xx, 1, z, y]
                both = (
                    jnp.where(left, even, pltpu.roll(odd, 64, 1)),
                    jnp.where(left, pltpu.roll(even, 64, 1), odd),
                )
                for which, full in enumerate(both):
                    hi = full.astype(BF16)
                    lo = (full - hi.astype(F32)).astype(BF16)
                    at = pl.ds(pl.multiple_of(512 * which + 32 * (4 * z + y) + first, 16), 16)
                    xh[at, 128 * xx : 128 * xx + 128] = hi
                    xh[at, 512 + 128 * xx : 640 + 128 * xx] = lo

    def sort_rows():
        lane = lax.broadcasted_iota(I32, (8, 128), 1)
        sub = lax.broadcasted_iota(I32, (8, 128), 0)

        def take(m, carry):
            tile = gi[here[0], core, m // 4, m % 4]
            for u in range(4):
                t = tile if u == 0 else pltpu.roll(tile, 128 - 16 * u, 1)
                row = 32 * m + 8 * u + sub
                live = jnp.where((lane >= 8) & (lane < 16) & (t != 248.0), 1.0, 0.0)
                count = jnp.sum(live, axis=1, keepdims=True)
                e = t * 0.125
                h = jnp.floor(e * 0.5)
                low = pltpu.roll(e - 2.0 * h, 16, 1)
                value = jnp.where(lane < 16, h, jnp.where(lane < 32, low, 0.0))
                value = jnp.where(lane == 32, lax.shift_right_logical(row, 1).astype(F32), value)
                value = jnp.where(lane == 33, (row & 1).astype(F32), value)
                value = jnp.where(lane == 34, count, value)
                at = pl.ds(pl.multiple_of(32 * m + 8 * u, 8), 8)
                listed[at, :] = value
                keys[at, :] = count * 512.0 + (511 - row).astype(F32)
            return carry

        lax.fori_loop(0, 16, take, 0)
        key_row = jnp.transpose(keys[...])[0:1, :]

        def above(b, total):
            key = keys[pl.ds(pl.multiple_of(8 * b, 8), 8), :]
            key = jnp.concatenate([key, key, key, key], axis=1)
            return total + jnp.where(key > key_row, 1.0, 0.0)

        total = lax.fori_loop(0, 64, above, jnp.zeros((8, 512), F32))
        place = jnp.sum(total, axis=0, keepdims=True).astype(I32)
        chosen = jnp.where(lax.broadcasted_iota(I32, (512, 512), 0) == place, 1.0, 0.0).astype(BF16)
        keys[...] = jnp.dot(chosen, listed[...].astype(BF16), preferred_element_type=F32)

        lane64 = lax.broadcasted_iota(I32, (64, 128), 1)
        flat, names = None, None
        for v in range(8):
            t = keys[pl.ds(v, 64, stride=8), :]
            slots = 16.0 * t + 8.0 * pltpu.roll(t, 112, 1)
            name = 2.0 * t + pltpu.roll(t, 127, 1)
            if v == 0:
                flat = slots
                names = pltpu.roll(name, 96, 1)
                reach = jnp.where(t[:, 34:35] >= lane64.astype(F32), 1.0, 0.0)
                bounds[...] = jnp.broadcast_to(jnp.sum(reach, axis=0, keepdims=True), (8, 128)).astype(I32)
            else:
                flat = jnp.where(lane64 >= 16 * v, pltpu.roll(slots, 16 * v, 1), flat)
                names = jnp.where(lane64 >= v, pltpu.roll(name, 96 + v, 1), names)
        lists[...] = flat.astype(I32)
        ids[...] = names.astype(I32)

    def arrived(back, start):
        for n in range(start, 3):
            wait(parts[n][0].at[0, 0], rp.at[n, back])

    def split_both(back):
        split(ga, moved(1, (4 - back) % 4)[1], True, 0)
        split(gc, moved(2, (4 - back) % 4)[2], False, 16)

    for n, (g, slab, order) in enumerate(parts):
        plane = box(g, here, order[:2])
        send(plane, plane, sp.at[n], rp.at[n, 0], partner)
    sort_rows()
    arrived(0, 0)
    split_both(0)
    for back in (1, 3, 2):
        for n, (g, slab, order) in enumerate(parts):
            wait(g.at[0, 0], r3.at[n, back - 1])
            plane = box(g, moved(order[2], 4 - back), order[:2])
            send(plane, plane, sp.at[n], rp.at[n, back], partner)
    for back in (1, 3):
        arrived(back, 1)
        split_both(back)
    for back in (1, 3, 2):
        wait(gi.at[0, 0], rp.at[0, back])

    lane8 = lax.broadcasted_iota(I32, (8, 128), 1)
    zz, yy = here[1], here[2]
    for half in range(2):
        for which in range(2):
            full = None
            for y in range(4):
                tile = gi[zz, yy // 2, 2 * (yy % 2) + half, y]
                turn = (32 * (y - 2 - which)) % 128
                t = tile if turn == 0 else pltpu.roll(tile, turn, 1)
                full = t if full is None else jnp.where(lane8 >= 32 * y, t, full)
            pq[8 * which : 8 * which + 8, 128 * half : 128 * half + 128] = full.astype(I32)

    place = lax.broadcasted_iota(I32, (512, 256), 0)

    def columns(n, carry):
        hot[n] = jnp.where(place == pq[pl.ds(n, 1), :], 1.0, 0.0).astype(BF16)
        return carry

    lax.fori_loop(0, 16, columns, 0)
    arrived(2, 1)
    split_both(2)
    for n, (g, slab, order) in enumerate(parts):
        wait(g.at[0, 0, 0, 0:3], s1.at[n, 0])
        wait(g.at[0, 0, 0:3], s1.at[n, 1])
        wait(g.at[0:3, 0], s3.at[n])
        wait(g.at[:, 0], sp.at[n])


def table_kernel(xh, hot, lists, ids, bounds, out_ref, sm, names, ends, tx, acc, rows_out, sem):
    to_scalar = [
        pltpu.make_async_copy(a, b, sem.at[n])
        for n, (a, b) in enumerate(((lists, sm), (ids, names), (bounds, ends)))
    ]
    for copy in to_scalar:
        copy.start()

    def tables(nn, *units):
        for extra in range(2):
            n = 2 * nn + extra
            which, l = n // 8, n % 8
            for unit in range(2):
                sums = units[2 * extra + unit]
                rows = pl.ds(pl.multiple_of(512 * which + 256 * unit, 256), 256)
                for half in range(2):
                    pltpu.matmul_push_rhs(hot[n, 256 * half : 256 * half + 256, :], half, unit)
                for half in range(2):
                    pltpu.matmul_acc_lhs(sums, xh[rows, 256 * half : 256 * half + 256], load_staged_rhs=half)
                    pltpu.matmul_acc_lhs(sums, xh[rows, 512 + 256 * half : 768 + 256 * half])
            for unit in range(2):
                t = pltpu.matmul_pop(units[2 * extra + unit])
                tx[pl.ds(8208 * which + 2048 * unit + l, 256, stride=8), :] = t[:, 0:128]
                tx[pl.ds(8208 * which + 4104 + 2048 * unit + l, 256, stride=8), :] = t[:, 128:256]

    def scoped(nn, carry):
        pl.run_scoped(functools.partial(tables, nn), *(pltpu.ACC(unit)((256, 256), F32) for unit in (0, 1, 0, 1)))
        return carry

    lax.fori_loop(0, 8, scoped, 0)
    for copy in to_scalar:
        copy.wait()

    sub = lax.broadcasted_iota(I32, (8, 128), 0)
    low4, low2, low1 = sub < 4, sub % 4 < 2, sub % 2 < 1

    def folded(a):
        b = [
            jnp.where(low4, a[v], a[v + 4]) + pltpu.roll(jnp.where(low4, a[v + 4], a[v]), 4, 0)
            for v in range(4)
        ]
        d = [
            jnp.where(low2, b[v], pltpu.roll(b[v + 2], 2, 0))
            + jnp.where(low2, pltpu.roll(b[v], 6, 0), b[v + 2])
            for v in range(2)
        ]
        return jnp.where(low1, d[0], pltpu.roll(d[1], 1, 0)) + jnp.where(
            low1, pltpu.roll(d[0], 7, 0), d[1]
        )

    def fold_group(n, slot):
        for half in range(2):
            here = [acc[pl.ds(pl.multiple_of(128 * slot + 64 * half + 8 * v, 8), 8), :] for v in range(8)]
            sums = folded(here)
            for v in range(8):
                rows_out[pl.ds(512 * half + names[n, v], 1), :] = sums[v : v + 1, :]

    def group(count, n, carry):
        slot = n % 2
        fold_group(jnp.maximum(n - 1, 0), 1 - slot)
        for v in range(8):
            a0, a1 = None, None
            for k in range(count):
                p = pl.multiple_of(sm[n, 16 * v + k], 8)
                q = pl.multiple_of(sm[n, 16 * v + 8 + k], 8)
                s0 = tx[pl.ds(q, 8), :] * tx[pl.ds(p + 8208, 8), :]
                s1 = tx[pl.ds(q + 4104, 8), :] * tx[pl.ds(p + 12312, 8), :]
                a0 = s0 if a0 is None else a0 + s0
                a1 = s1 if a1 is None else a1 + s1
            acc[pl.ds(pl.multiple_of(128 * slot + 8 * v, 8), 8), :] = a0
            acc[pl.ds(pl.multiple_of(128 * slot + 64 + 8 * v, 8), 8), :] = a1
        return carry

    first = jnp.int32(0)
    for count in range(8, 0, -1):
        last = ends[0, count] if count > 1 else jnp.int32(64)
        lax.fori_loop(first, last, functools.partial(group, count), 0)
        first = last
    fold_group(63, 1)
    halves = [
        pltpu.make_async_copy(
            rows_out.at[512 * half : 512 * half + 512], out_ref.at[:, 128 * half : 128 * half + 128], sem.at[half]
        )
        for half in range(2)
    ]
    for copy in halves:
        copy.start()
    for copy in halves:
        copy.wait()


def gather(x, w, pos, cnt):
    dma = pltpu.SemaphoreType.DMA
    vmem = pltpu.VMEM
    return pl.pallas_call(
        gather_kernel,
        out_shape=(
            jax.ShapeDtypeStruct((1024, 1152), BF16),
            jax.ShapeDtypeStruct((16, 512, 256), BF16),
            jax.ShapeDtypeStruct((64, 128), I32),
            jax.ShapeDtypeStruct((64, 128), I32),
            jax.ShapeDtypeStruct((8, 128), I32),
        ),
        in_specs=[pl.BlockSpec(memory_space=pltpu.HBM)] * 4,
        out_specs=tuple(pl.BlockSpec(memory_space=vmem) for n in range(5)),
        scratch_shapes=[
            vmem((4, 2, 4, 4, 8, 128), F32),
            vmem((4, 2, 4, 4, 16, 128), F32),
            vmem((4, 2, 4, 4, 16, 128), F32),
            vmem((512, 128), F32),
            vmem((512, 128), F32),
            vmem((31, 62), F32),
            vmem((31, 62), F32),
            vmem((16, 32), I32),
            vmem((32,), I32),
            vmem((16, 128), F32),
            vmem((16, 128), F32),
            vmem((8, 128), F32),
            vmem((16, 256), I32),
            dma((7,)),
            dma((3, 2)),
            dma((3,)),
            dma((3,)),
            dma((3, 4)),
            dma((3, 3)),
            dma((3, 4)),
        ],
        compiler_params=pltpu.CompilerParams(collective_id=0, has_side_effects=True, vmem_limit_bytes=16 << 20),
        name="gather",
    )(x, w, pos, cnt)


def tabled(*gathered):
    return pl.pallas_call(
        table_kernel,
        out_shape=jax.ShapeDtypeStruct((512, 256), F32),
        in_specs=[pl.BlockSpec(memory_space=pltpu.VMEM)] * 5,
        out_specs=pl.BlockSpec(memory_space=pl.ANY),
        scratch_shapes=[
            pltpu.SMEM((64, 128), I32),
            pltpu.SMEM((64, 128), I32),
            pltpu.SMEM((8, 128), I32),
            pltpu.VMEM((16416, 128), F32),
            pltpu.VMEM((256, 128), F32),
            pltpu.VMEM((1024, 128), F32),
            pltpu.SemaphoreType.DMA((3,)),
        ],
        compiler_params=pltpu.CompilerParams(vmem_limit_bytes=40 << 20),
        name="tables",
    )(*gathered)


def shards(moment_x, zinv, positions, entry_count):
    ins = (moment_x.T, zinv.T, positions.T, entry_count)
    return tabled(*gather(*(pltpu.with_memory_space_constraint(a, pltpu.HBM) for a in ins)))


def solution(mesh):
    return jax.shard_map(
        shards,
        mesh=mesh,
        in_specs=(P("row", "col"), P("row", "col"), P(("row", "col"), None), P(("row", "col"))),
        out_specs=P("row", "col"),
        check_vma=False,
    )
```

```python
import functools

import jax
import jax.numpy as jnp
from jax import lax
from jax.experimental import pallas as pl
from jax.experimental.pallas import tpu as pltpu
from jax.sharding import PartitionSpec as P

MESH = pl.DeviceIdType.MESH
F32 = jnp.float32
BF16 = jnp.bfloat16
I32 = jnp.int32


def padded(v, part, factor, pad):
    return v + pad * lax.shift_right_logical(v * factor, 16)


def gather_kernel(
    x_in, w_in, pos_in, cnt_in, xh, hot, lists, ids, bounds,
    gi, ga, gc, listed, keys, x_ref, w_ref, pos_ref, cnt_ref, slab_a, slab_c, slab_i, pq, loc, s1, s3, sp, r1, r3, rp,
):
    r = lax.axis_index("row")
    c = lax.axis_index("col")
    core = r % 2
    here = (r // 2, c // 4, c % 4)
    ins = [
        pltpu.make_async_copy(a, b, loc.at[n])
        for n, (a, b) in enumerate(((x_in, x_ref), (w_in, w_ref), (pos_in, pos_ref), (cnt_in, cnt_ref)))
    ]
    for copy in ins:
        copy.start()

    def moved(axis, offset):
        at = list(here)
        at[axis] = (at[axis] + offset) % 4
        return at

    def device(at):
        return (2 * at[0] + core, 4 * at[1] + at[2])

    partner = (r + 1 - 2 * core, c)
    barrier = pltpu.get_barrier_semaphore()
    near = [
        (dx, dz, dy)
        for dx in range(4)
        for dz in range(4)
        for dy in range(4)
        if dx * dz * dy == 0 and dx + dz + dy > 0
    ]
    near.sort(key=lambda o: -sum(min(v, 4 - v) for v in o))

    def shifted(offsets):
        return [(at + o) % 4 if o else at for at, o in zip(here, offsets)]

    for offsets in near:
        pl.semaphore_signal(barrier, inc=1, device_id=device(shifted(offsets)), device_id_type=MESH)
    pl.semaphore_signal(barrier, inc=1, device_id=partner, device_id_type=MESH)

    for ref in (slab_a, slab_c, slab_i):
        ref[...] = jnp.zeros_like(ref)
    for copy in ins:
        copy.wait()
    for lanes, src in ((0, x_ref), (64, w_ref)):
        slab_a[:, lanes : lanes + 62] = src[0:16, :]
        slab_c[0:15, lanes : lanes + 62] = src[16:31, :]

    pos = pos_ref[...]
    live = lax.broadcasted_iota(I32, (16, 32), 0) % 8 < cnt_ref[...].reshape(1, 32)
    cols = jnp.where(live, padded(pos, 62, 1058, 2), 62).astype(F32)
    rows = jnp.where(live, padded(pos, 31, 2115, 1), 31).astype(F32) * 8.0
    rows = jnp.transpose(rows)
    for u in range(4):
        slab_i[:, 16 * u : 16 * u + 16] = rows[8 * u : 8 * u + 8, :]
    slab_i[:, 64:96] = cols[0:8, :]
    slab_i[:, 96:128] = cols[8:16, :]

    every = pl.ds(0, 4)
    parts = ((gi, slab_i, (2, 1, 0)), (ga, slab_a, (2, 0, 1)), (gc, slab_c, (1, 0, 2)))

    def box(g, at, open_axes=()):
        index = [every if axis in open_axes else at[axis] for axis in range(3)]
        return g.at[index[0], core, index[1], index[2]]

    own = [
        pltpu.make_async_copy(slab, box(g, here), loc.at[4 + n]) for n, (g, slab, order) in enumerate(parts)
    ]
    for copy in own:
        copy.start()
    pl.semaphore_wait(barrier, len(near) + 1)

    def send(src, dst, send_sem, recv_sem, to):
        pltpu.make_async_remote_copy(
            src, dst, send_sem, recv_sem, device_id=to, device_id_type=MESH
        ).start()

    def wait(ref, sem):
        pltpu.make_async_copy(ref, ref, sem).wait()

    for step in (0, 1, 3, 2):
        for side in (2, 1, 3, 0):
            for n, (g, slab, order) in enumerate(parts):
                if step or side:
                    offsets = [0, 0, 0]
                    offsets[order[0]], offsets[order[1]] = step, side
                    send(slab, box(g, here), s1.at[n, min(step, 1)], r1.at[n, step], device(shifted(offsets)))
    for copy in own:
        copy.wait()
    for back in (0, 1, 3, 2):
        for n, (g, slab, order) in enumerate(parts):
            wait(g.at[0, 0, 0, 0 : 4 if back else 3], r1.at[n, back])
            line = box(g, moved(order[0], (4 - back) % 4), order[1:2])
            for offset in (1, 3, 2):
                send(line, line, s3.at[n], r3.at[n, offset - 1], device(moved(order[2], offset)))
    left = lax.broadcasted_iota(I32, (16, 128), 1) < 64

    def split(g, plane, along_z, first):
        for step in range(4):
            z, y = (plane, step) if along_z else (step, plane)
            for xx in range(4):
                even, odd = g[xx, 0, z, y], g[xx, 1, z, y]
                both = (
                    jnp.where(left, even, pltpu.roll(odd, 64, 1)),
                    jnp.where(left, pltpu.roll(even, 64, 1), odd),
                )
                for which, full in enumerate(both):
                    hi = full.astype(BF16)
                    lo = (full - hi.astype(F32)).astype(BF16)
                    at = pl.ds(pl.multiple_of(512 * which + 32 * (4 * z + y) + first, 16), 16)
                    xh[at, 128 * xx : 128 * xx + 128] = hi
                    xh[at, 512 + 128 * xx : 640 + 128 * xx] = lo

    def sort_rows():
        lane = lax.broadcasted_iota(I32, (8, 128), 1)
        sub = lax.broadcasted_iota(I32, (8, 128), 0)

        def take(m, carry):
            tile = gi[here[0], core, m // 4, m % 4]
            for u in range(4):
                t = tile if u == 0 else pltpu.roll(tile, 128 - 16 * u, 1)
                row = 32 * m + 8 * u + sub
                live = jnp.where((lane >= 8) & (lane < 16) & (t != 248.0), 1.0, 0.0)
                count = jnp.sum(live, axis=1, keepdims=True)
                e = t * 0.125
                h = jnp.floor(e * 0.5)
                low = pltpu.roll(e - 2.0 * h, 16, 1)
                value = jnp.where(lane < 16, h, jnp.where(lane < 32, low, 0.0))
                value = jnp.where(lane == 32, lax.shift_right_logical(row, 1).astype(F32), value)
                value = jnp.where(lane == 33, (row & 1).astype(F32), value)
                value = jnp.where(lane == 34, count, value)
                at = pl.ds(pl.multiple_of(32 * m + 8 * u, 8), 8)
                listed[at, :] = value
                keys[at, :] = count * 512.0 + (511 - row).astype(F32)
            return carry

        lax.fori_loop(0, 16, take, 0)
        key_row = jnp.transpose(keys[...])[0:1, :]

        def above(b, total):
            key = keys[pl.ds(pl.multiple_of(8 * b, 8), 8), :]
            key = jnp.concatenate([key, key, key, key], axis=1)
            return total + jnp.where(key > key_row, 1.0, 0.0)

        total = lax.fori_loop(0, 64, above, jnp.zeros((8, 512), F32))
        place = jnp.sum(total, axis=0, keepdims=True).astype(I32)
        chosen = jnp.where(lax.broadcasted_iota(I32, (512, 512), 0) == place, 1.0, 0.0).astype(BF16)
        keys[...] = jnp.dot(chosen, listed[...].astype(BF16), preferred_element_type=F32)

        lane64 = lax.broadcasted_iota(I32, (64, 128), 1)
        flat, names = None, None
        for v in range(8):
            t = keys[pl.ds(v, 64, stride=8), :]
            slots = 16.0 * t + 8.0 * pltpu.roll(t, 112, 1)
            name = 2.0 * t + pltpu.roll(t, 127, 1)
            if v == 0:
                flat = slots
                names = pltpu.roll(name, 96, 1)
                reach = jnp.where(t[:, 34:35] >= lane64.astype(F32), 1.0, 0.0)
                bounds[...] = jnp.broadcast_to(jnp.sum(reach, axis=0, keepdims=True), (8, 128)).astype(I32)
            else:
                flat = jnp.where(lane64 >= 16 * v, pltpu.roll(slots, 16 * v, 1), flat)
                names = jnp.where(lane64 >= v, pltpu.roll(name, 96 + v, 1), names)
        lists[...] = flat.astype(I32)
        ids[...] = names.astype(I32)

    def arrived(back, start):
        for n in range(start, 3):
            wait(parts[n][0].at[0, 0], rp.at[n, back])

    def split_both(back):
        split(ga, moved(1, (4 - back) % 4)[1], True, 0)
        split(gc, moved(2, (4 - back) % 4)[2], False, 16)

    for n, (g, slab, order) in enumerate(parts):
        plane = box(g, here, order[:2])
        send(plane, plane, sp.at[n], rp.at[n, 0], partner)
    sort_rows()
    arrived(0, 0)
    split_both(0)
    for back in (1, 3, 2):
        for n, (g, slab, order) in enumerate(parts):
            wait(g.at[0, 0], r3.at[n, back - 1])
            plane = box(g, moved(order[2], 4 - back), order[:2])
            send(plane, plane, sp.at[n], rp.at[n, back], partner)
    for back in (1, 3):
        arrived(back, 1)
        split_both(back)
    for back in (1, 3, 2):
        wait(gi.at[0, 0], rp.at[0, back])

    lane8 = lax.broadcasted_iota(I32, (8, 128), 1)
    zz, yy = here[1], here[2]
    for half in range(2):
        for which in range(2):
            full = None
            for y in range(4):
                tile = gi[zz, yy // 2, 2 * (yy % 2) + half, y]
                turn = (32 * (y - 2 - which)) % 128
                t = tile if turn == 0 else pltpu.roll(tile, turn, 1)
                full = t if full is None else jnp.where(lane8 >= 32 * y, t, full)
            pq[8 * which : 8 * which + 8, 128 * half : 128 * half + 128] = full.astype(I32)

    place = lax.broadcasted_iota(I32, (512, 256), 0)

    def columns(n, carry):
        hot[n] = jnp.where(place == pq[pl.ds(n, 1), :], 1.0, 0.0).astype(BF16)
        return carry

    lax.fori_loop(0, 16, columns, 0)
    arrived(2, 1)
    split_both(2)
    for n, (g, slab, order) in enumerate(parts):
        wait(g.at[0, 0, 0, 0:3], s1.at[n, 0])
        wait(g.at[0, 0, 0:3], s1.at[n, 1])
        wait(g.at[0:3, 0], s3.at[n])
        wait(g.at[:, 0], sp.at[n])


def table_kernel(xh, hot, lists, ids, bounds, out_ref, sm, names, ends, tx, acc, rows_out, sem):
    to_scalar = [
        pltpu.make_async_copy(a, b, sem.at[n])
        for n, (a, b) in enumerate(((lists, sm), (ids, names), (bounds, ends)))
    ]
    for copy in to_scalar:
        copy.start()

    def multiply(n, sums):
        for unit in range(2):
            rows = pl.ds(pl.multiple_of(512 * (n // 8) + 256 * unit, 256), 256)
            for half in range(2):
                pltpu.matmul_push_rhs(hot[n, 256 * half : 256 * half + 256, :], half, unit)
            for half in range(2):
                pltpu.matmul_acc_lhs(sums[unit], xh[rows, 256 * half : 256 * half + 256], load_staged_rhs=half)
                pltpu.matmul_acc_lhs(sums[unit], xh[rows, 512 + 256 * half : 768 + 256 * half])

    def store(n, sums):
        base = 8208 * (n // 8) + n % 8
        for unit in range(2):
            t = pltpu.matmul_pop(sums[unit])
            tx[pl.ds(base + 2048 * unit, 256, stride=8), :] = t[:, 0:128]
            tx[pl.ds(base + 4104 + 2048 * unit, 256, stride=8), :] = t[:, 128:256]

    def tables(*units):
        first, second = units[0:2], units[2:4]
        multiply(jnp.int32(0), first)

        def pair(nn, carry):
            multiply(2 * nn + 1, second)
            store(2 * nn, first)
            multiply(2 * nn + 2, first)
            store(2 * nn + 1, second)
            return carry

        lax.fori_loop(0, 7, pair, 0)
        multiply(jnp.int32(15), second)
        store(14, first)
        store(15, second)

    pl.run_scoped(tables, *(pltpu.ACC(unit)((256, 256), F32) for unit in (0, 1, 0, 1)))
    for copy in to_scalar:
        copy.wait()

    sub = lax.broadcasted_iota(I32, (8, 128), 0)
    low4, low2, low1 = sub < 4, sub % 4 < 2, sub % 2 < 1

    def folded(a):
        b = [
            jnp.where(low4, a[v], a[v + 4]) + pltpu.roll(jnp.where(low4, a[v + 4], a[v]), 4, 0)
            for v in range(4)
        ]
        d = [
            jnp.where(low2, b[v], pltpu.roll(b[v + 2], 2, 0))
            + jnp.where(low2, pltpu.roll(b[v], 6, 0), b[v + 2])
            for v in range(2)
        ]
        return jnp.where(low1, d[0], pltpu.roll(d[1], 1, 0)) + jnp.where(
            low1, pltpu.roll(d[0], 7, 0), d[1]
        )

    def fold_group(n, slot):
        for half in range(2):
            here = [acc[pl.ds(pl.multiple_of(128 * slot + 64 * half + 8 * v, 8), 8), :] for v in range(8)]
            sums = folded(here)
            for v in range(8):
                rows_out[pl.ds(512 * half + names[n, v], 1), :] = sums[v : v + 1, :]

    def group(count, n, carry):
        slot = n % 2
        fold_group(jnp.maximum(n - 1, 0), 1 - slot)
        for v in range(8):
            a0, a1 = None, None
            for k in range(count):
                p = pl.multiple_of(sm[n, 16 * v + k], 8)
                q = pl.multiple_of(sm[n, 16 * v + 8 + k], 8)
                s0 = tx[pl.ds(q, 8), :] * tx[pl.ds(p + 8208, 8), :]
                s1 = tx[pl.ds(q + 4104, 8), :] * tx[pl.ds(p + 12312, 8), :]
                a0 = s0 if a0 is None else a0 + s0
                a1 = s1 if a1 is None else a1 + s1
            acc[pl.ds(pl.multiple_of(128 * slot + 8 * v, 8), 8), :] = a0
            acc[pl.ds(pl.multiple_of(128 * slot + 64 + 8 * v, 8), 8), :] = a1
        return carry

    first = jnp.int32(0)
    for count in range(8, 0, -1):
        last = ends[0, count] if count > 1 else jnp.int32(64)
        lax.fori_loop(first, last, functools.partial(group, count), 0)
        first = last
    fold_group(63, 1)
    halves = [
        pltpu.make_async_copy(
            rows_out.at[512 * half : 512 * half + 512], out_ref.at[:, 128 * half : 128 * half + 128], sem.at[half]
        )
        for half in range(2)
    ]
    for copy in halves:
        copy.start()
    for copy in halves:
        copy.wait()


def gather(x, w, pos, cnt):
    dma = pltpu.SemaphoreType.DMA
    vmem = pltpu.VMEM
    return pl.pallas_call(
        gather_kernel,
        out_shape=(
            jax.ShapeDtypeStruct((1024, 1152), BF16),
            jax.ShapeDtypeStruct((16, 512, 256), BF16),
            jax.ShapeDtypeStruct((64, 128), I32),
            jax.ShapeDtypeStruct((64, 128), I32),
            jax.ShapeDtypeStruct((8, 128), I32),
        ),
        in_specs=[pl.BlockSpec(memory_space=pltpu.HBM)] * 4,
        out_specs=tuple(pl.BlockSpec(memory_space=vmem) for n in range(5)),
        scratch_shapes=[
            vmem((4, 2, 4, 4, 8, 128), F32),
            vmem((4, 2, 4, 4, 16, 128), F32),
            vmem((4, 2, 4, 4, 16, 128), F32),
            vmem((512, 128), F32),
            vmem((512, 128), F32),
            vmem((31, 62), F32),
            vmem((31, 62), F32),
            vmem((16, 32), I32),
            vmem((32,), I32),
            vmem((16, 128), F32),
            vmem((16, 128), F32),
            vmem((8, 128), F32),
            vmem((16, 256), I32),
            dma((7,)),
            dma((3, 2)),
            dma((3,)),
            dma((3,)),
            dma((3, 4)),
            dma((3, 3)),
            dma((3, 4)),
        ],
        compiler_params=pltpu.CompilerParams(collective_id=0, has_side_effects=True, vmem_limit_bytes=16 << 20),
        name="gather",
    )(x, w, pos, cnt)


def tabled(*gathered):
    return pl.pallas_call(
        table_kernel,
        out_shape=jax.ShapeDtypeStruct((512, 256), F32),
        in_specs=[pl.BlockSpec(memory_space=pltpu.VMEM)] * 5,
        out_specs=pl.BlockSpec(memory_space=pl.ANY),
        scratch_shapes=[
            pltpu.SMEM((64, 128), I32),
            pltpu.SMEM((64, 128), I32),
            pltpu.SMEM((8, 128), I32),
            pltpu.VMEM((16416, 128), F32),
            pltpu.VMEM((256, 128), F32),
            pltpu.VMEM((1024, 128), F32),
            pltpu.SemaphoreType.DMA((3,)),
        ],
        compiler_params=pltpu.CompilerParams(vmem_limit_bytes=40 << 20),
        name="tables",
    )(*gathered)


def shards(moment_x, zinv, positions, entry_count):
    ins = (moment_x.T, zinv.T, positions.T, entry_count)
    return tabled(*gather(*(pltpu.with_memory_space_constraint(a, pltpu.HBM) for a in ins)))


def solution(mesh):
    return jax.shard_map(
        shards,
        mesh=mesh,
        in_specs=(P("row", "col"), P("row", "col"), P(("row", "col"), None), P(("row", "col"))),
        out_specs=P("row", "col"),
        check_vma=False,
    )
```

```python
import functools

import jax
import jax.numpy as jnp
from jax import lax
from jax.experimental import pallas as pl
from jax.experimental.pallas import tpu as pltpu
from jax.sharding import PartitionSpec as P

MESH = pl.DeviceIdType.MESH
F32 = jnp.float32
BF16 = jnp.bfloat16
I32 = jnp.int32


def padded(v, part, factor, pad):
    return v + pad * lax.shift_right_logical(v * factor, 16)


def gather_kernel(
    x_in, w_in, pos_in, cnt_in, xh, hot, lists, ids, bounds,
    gi, ga, gc, listed, keys, x_ref, w_ref, pos_ref, cnt_ref, slab_a, slab_c, slab_i, pq, loc, s1, s3, sp, r1, r3, rp,
):
    r = lax.axis_index("row")
    c = lax.axis_index("col")
    core = r % 2
    here = (r // 2, c // 4, c % 4)
    ins = [
        pltpu.make_async_copy(a, b, loc.at[n])
        for n, (a, b) in enumerate(((x_in, x_ref), (w_in, w_ref), (pos_in, pos_ref), (cnt_in, cnt_ref)))
    ]
    for copy in ins:
        copy.start()

    def moved(axis, offset):
        at = list(here)
        at[axis] = (at[axis] + offset) % 4
        return at

    def device(at):
        return (2 * at[0] + core, 4 * at[1] + at[2])

    partner = (r + 1 - 2 * core, c)
    barrier = pltpu.get_barrier_semaphore()
    near = [
        (dx, dz, dy)
        for dx in range(4)
        for dz in range(4)
        for dy in range(4)
        if dx * dz * dy == 0 and dx + dz + dy > 0
    ]
    near.sort(key=lambda o: -sum(min(v, 4 - v) for v in o))

    def shifted(offsets):
        return [(at + o) % 4 if o else at for at, o in zip(here, offsets)]

    for offsets in near:
        pl.semaphore_signal(barrier, inc=1, device_id=device(shifted(offsets)), device_id_type=MESH)
    pl.semaphore_signal(barrier, inc=1, device_id=partner, device_id_type=MESH)

    for ref in (slab_a, slab_c, slab_i):
        ref[...] = jnp.zeros_like(ref)
    for copy in ins:
        copy.wait()
    for lanes, src in ((0, x_ref), (64, w_ref)):
        slab_a[:, lanes : lanes + 62] = src[0:16, :]
        slab_c[0:15, lanes : lanes + 62] = src[16:31, :]

    pos = pos_ref[...]
    live = lax.broadcasted_iota(I32, (16, 32), 0) % 8 < cnt_ref[...].reshape(1, 32)
    cols = jnp.where(live, padded(pos, 62, 1058, 2), 62).astype(F32)
    rows = jnp.where(live, padded(pos, 31, 2115, 1), 31).astype(F32) * 8.0
    rows = jnp.transpose(rows)
    for u in range(4):
        slab_i[:, 16 * u : 16 * u + 16] = rows[8 * u : 8 * u + 8, :]
    slab_i[:, 64:96] = cols[0:8, :]
    slab_i[:, 96:128] = cols[8:16, :]

    every = pl.ds(0, 4)
    parts = ((gi, slab_i, (2, 1, 0)), (ga, slab_a, (2, 0, 1)), (gc, slab_c, (1, 0, 2)))

    def box(g, at, open_axes=()):
        index = [every if axis in open_axes else at[axis] for axis in range(3)]
        return g.at[index[0], core, index[1], index[2]]

    own = [
        pltpu.make_async_copy(slab, box(g, here), loc.at[4 + n]) for n, (g, slab, order) in enumerate(parts)
    ]
    for copy in own:
        copy.start()
    pl.semaphore_wait(barrier, len(near) + 1)

    def send(src, dst, send_sem, recv_sem, to):
        pltpu.make_async_remote_copy(
            src, dst, send_sem, recv_sem, device_id=to, device_id_type=MESH
        ).start()

    def wait(ref, sem):
        pltpu.make_async_copy(ref, ref, sem).wait()

    for step in (0, 1, 3, 2):
        for side in (2, 1, 3, 0):
            for n, (g, slab, order) in enumerate(parts):
                if step or side:
                    offsets = [0, 0, 0]
                    offsets[order[0]], offsets[order[1]] = step, side
                    send(slab, box(g, here), s1.at[n, min(step, 1)], r1.at[n, step], device(shifted(offsets)))
    for copy in own:
        copy.wait()
    for back in (0, 1, 3, 2):
        for n, (g, slab, order) in enumerate(parts):
            wait(g.at[0, 0, 0, 0 : 4 if back else 3], r1.at[n, back])
            line = box(g, moved(order[0], (4 - back) % 4), order[1:2])
            for offset in (2, 1, 3):
                send(line, line, s3.at[n], r3.at[n, offset - 1], device(moved(order[2], offset)))
    left = lax.broadcasted_iota(I32, (16, 128), 1) < 64

    def split(g, plane, along_z, first):
        for step in range(4):
            z, y = (plane, step) if along_z else (step, plane)
            for xx in range(4):
                even, odd = g[xx, 0, z, y], g[xx, 1, z, y]
                both = (
                    jnp.where(left, even, pltpu.roll(odd, 64, 1)),
                    jnp.where(left, pltpu.roll(even, 64, 1), odd),
                )
                for which, full in enumerate(both):
                    hi = full.astype(BF16)
                    lo = (full - hi.astype(F32)).astype(BF16)
                    at = pl.ds(pl.multiple_of(512 * which + 32 * (4 * z + y) + first, 16), 16)
                    xh[at, 128 * xx : 128 * xx + 128] = hi
                    xh[at, 512 + 128 * xx : 640 + 128 * xx] = lo

    def sort_rows():
        lane = lax.broadcasted_iota(I32, (8, 128), 1)
        sub = lax.broadcasted_iota(I32, (8, 128), 0)

        def take(m, carry):
            tile = gi[here[0], core, m // 4, m % 4]
            for u in range(4):
                t = tile if u == 0 else pltpu.roll(tile, 128 - 16 * u, 1)
                row = 32 * m + 8 * u + sub
                live = jnp.where((lane >= 8) & (lane < 16) & (t != 248.0), 1.0, 0.0)
                count = jnp.sum(live, axis=1, keepdims=True)
                e = t * 0.125
                h = jnp.floor(e * 0.5)
                low = pltpu.roll(e - 2.0 * h, 16, 1)
                value = jnp.where(lane < 16, h, jnp.where(lane < 32, low, 0.0))
                value = jnp.where(lane == 32, lax.shift_right_logical(row, 1).astype(F32), value)
                value = jnp.where(lane == 33, (row & 1).astype(F32), value)
                value = jnp.where(lane == 34, count, value)
                at = pl.ds(pl.multiple_of(32 * m + 8 * u, 8), 8)
                listed[at, :] = value
                keys[at, :] = count * 512.0 + (511 - row).astype(F32)
            return carry

        lax.fori_loop(0, 16, take, 0)
        key_row = jnp.transpose(keys[...])[0:1, :]

        def above(b, total):
            key = keys[pl.ds(pl.multiple_of(8 * b, 8), 8), :]
            key = jnp.concatenate([key, key, key, key], axis=1)
            return total + jnp.where(key > key_row, 1.0, 0.0)

        total = lax.fori_loop(0, 64, above, jnp.zeros((8, 512), F32))
        place = jnp.sum(total, axis=0, keepdims=True).astype(I32)
        chosen = jnp.where(lax.broadcasted_iota(I32, (512, 512), 0) == place, 1.0, 0.0).astype(BF16)
        keys[...] = jnp.dot(chosen, listed[...].astype(BF16), preferred_element_type=F32)

        lane64 = lax.broadcasted_iota(I32, (64, 128), 1)
        flat, names = None, None
        for v in range(8):
            t = keys[pl.ds(v, 64, stride=8), :]
            slots = 16.0 * t + 8.0 * pltpu.roll(t, 112, 1)
            name = 2.0 * t + pltpu.roll(t, 127, 1)
            if v == 0:
                flat = slots
                names = pltpu.roll(name, 96, 1)
                reach = jnp.where(t[:, 34:35] >= lane64.astype(F32), 1.0, 0.0)
                bounds[...] = jnp.broadcast_to(jnp.sum(reach, axis=0, keepdims=True), (8, 128)).astype(I32)
            else:
                flat = jnp.where(lane64 >= 16 * v, pltpu.roll(slots, 16 * v, 1), flat)
                names = jnp.where(lane64 >= v, pltpu.roll(name, 96 + v, 1), names)
        lists[...] = flat.astype(I32)
        ids[...] = names.astype(I32)

    def arrived(back, start):
        for n in range(start, 3):
            wait(parts[n][0].at[0, 0], rp.at[n, back])

    def split_both(back):
        split(ga, moved(1, (4 - back) % 4)[1], True, 0)
        split(gc, moved(2, (4 - back) % 4)[2], False, 16)

    for n, (g, slab, order) in enumerate(parts):
        plane = box(g, here, order[:2])
        send(plane, plane, sp.at[n], rp.at[n, 0], partner)
    sort_rows()
    arrived(0, 0)
    split_both(0)
    for back in (1, 3, 2):
        for n, (g, slab, order) in enumerate(parts):
            wait(g.at[0, 0], r3.at[n, back - 1])
            plane = box(g, moved(order[2], 4 - back), order[:2])
            send(plane, plane, sp.at[n], rp.at[n, back], partner)
    for back in (1, 3):
        arrived(back, 1)
        split_both(back)
    for back in (1, 3, 2):
        wait(gi.at[0, 0], rp.at[0, back])

    lane8 = lax.broadcasted_iota(I32, (8, 128), 1)
    zz, yy = here[1], here[2]
    for half in range(2):
        for which in range(2):
            full = None
            for y in range(4):
                tile = gi[zz, yy // 2, 2 * (yy % 2) + half, y]
                turn = (32 * (y - 2 - which)) % 128
                t = tile if turn == 0 else pltpu.roll(tile, turn, 1)
                full = t if full is None else jnp.where(lane8 >= 32 * y, t, full)
            pq[8 * which : 8 * which + 8, 128 * half : 128 * half + 128] = full.astype(I32)

    place = lax.broadcasted_iota(I32, (512, 256), 0)

    def columns(n, carry):
        hot[n] = jnp.where(place == pq[pl.ds(n, 1), :], 1.0, 0.0).astype(BF16)
        return carry

    lax.fori_loop(0, 16, columns, 0)
    arrived(2, 1)
    split_both(2)
    for n, (g, slab, order) in enumerate(parts):
        wait(g.at[0, 0, 0, 0:3], s1.at[n, 0])
        wait(g.at[0, 0, 0:3], s1.at[n, 1])
        wait(g.at[0:3, 0], s3.at[n])
        wait(g.at[:, 0], sp.at[n])


def table_kernel(xh, hot, lists, ids, bounds, out_ref, sm, names, ends, tx, acc, rows_out, sem):
    to_scalar = [
        pltpu.make_async_copy(a, b, sem.at[n])
        for n, (a, b) in enumerate(((lists, sm), (ids, names), (bounds, ends)))
    ]
    for copy in to_scalar:
        copy.start()

    def multiply(n, sums):
        for unit in range(2):
            rows = pl.ds(pl.multiple_of(512 * (n // 8) + 256 * unit, 256), 256)
            for half in range(2):
                pltpu.matmul_push_rhs(hot[n, 256 * half : 256 * half + 256, :], half, unit)
            for half in range(2):
                pltpu.matmul_acc_lhs(sums[unit], xh[rows, 256 * half : 256 * half + 256], load_staged_rhs=half)
                pltpu.matmul_acc_lhs(sums[unit], xh[rows, 512 + 256 * half : 768 + 256 * half])

    def store(n, sums):
        base = 8208 * (n // 8) + n % 8
        for unit in range(2):
            t = pltpu.matmul_pop(sums[unit])
            tx[pl.ds(base + 2048 * unit, 256, stride=8), :] = t[:, 0:128]
            tx[pl.ds(base + 4104 + 2048 * unit, 256, stride=8), :] = t[:, 128:256]

    def tables(*units):
        first, second = units[0:2], units[2:4]
        multiply(jnp.int32(0), first)

        def pair(nn, carry):
            multiply(2 * nn + 1, second)
            store(2 * nn, first)
            multiply(2 * nn + 2, first)
            store(2 * nn + 1, second)
            return carry

        lax.fori_loop(0, 7, pair, 0)
        multiply(jnp.int32(15), second)
        store(14, first)
        store(15, second)

    pl.run_scoped(tables, *(pltpu.ACC(unit)((256, 256), F32) for unit in (0, 1, 0, 1)))
    for copy in to_scalar:
        copy.wait()

    sub = lax.broadcasted_iota(I32, (8, 128), 0)
    low4, low2, low1 = sub < 4, sub % 4 < 2, sub % 2 < 1

    def folded(a):
        b = [
            jnp.where(low4, a[v], a[v + 4]) + pltpu.roll(jnp.where(low4, a[v + 4], a[v]), 4, 0)
            for v in range(4)
        ]
        d = [
            jnp.where(low2, b[v], pltpu.roll(b[v + 2], 2, 0))
            + jnp.where(low2, pltpu.roll(b[v], 6, 0), b[v + 2])
            for v in range(2)
        ]
        return jnp.where(low1, d[0], pltpu.roll(d[1], 1, 0)) + jnp.where(
            low1, pltpu.roll(d[0], 7, 0), d[1]
        )

    def fold_group(n, slot):
        for half in range(2):
            here = [acc[pl.ds(pl.multiple_of(128 * slot + 64 * half + 8 * v, 8), 8), :] for v in range(8)]
            sums = folded(here)
            for v in range(8):
                rows_out[pl.ds(512 * half + names[n, v], 1), :] = sums[v : v + 1, :]

    def group(count, n, carry):
        slot = n % 2
        fold_group(jnp.maximum(n - 1, 0), 1 - slot)
        for v in range(8):
            a0, a1 = None, None
            for k in range(count):
                p = pl.multiple_of(sm[n, 16 * v + k], 8)
                q = pl.multiple_of(sm[n, 16 * v + 8 + k], 8)
                s0 = tx[pl.ds(q, 8), :] * tx[pl.ds(p + 8208, 8), :]
                s1 = tx[pl.ds(q + 4104, 8), :] * tx[pl.ds(p + 12312, 8), :]
                a0 = s0 if a0 is None else a0 + s0
                a1 = s1 if a1 is None else a1 + s1
            acc[pl.ds(pl.multiple_of(128 * slot + 8 * v, 8), 8), :] = a0
            acc[pl.ds(pl.multiple_of(128 * slot + 64 + 8 * v, 8), 8), :] = a1
        return carry

    first = jnp.int32(0)
    for count in range(8, 0, -1):
        last = ends[0, count] if count > 1 else jnp.int32(64)
        lax.fori_loop(first, last, functools.partial(group, count), 0)
        first = last
    fold_group(63, 1)
    halves = [
        pltpu.make_async_copy(
            rows_out.at[512 * half : 512 * half + 512], out_ref.at[:, 128 * half : 128 * half + 128], sem.at[half]
        )
        for half in range(2)
    ]
    for copy in halves:
        copy.start()
    for copy in halves:
        copy.wait()


def gather(x, w, pos, cnt):
    dma = pltpu.SemaphoreType.DMA
    vmem = pltpu.VMEM
    return pl.pallas_call(
        gather_kernel,
        out_shape=(
            jax.ShapeDtypeStruct((1024, 1152), BF16),
            jax.ShapeDtypeStruct((16, 512, 256), BF16),
            jax.ShapeDtypeStruct((64, 128), I32),
            jax.ShapeDtypeStruct((64, 128), I32),
            jax.ShapeDtypeStruct((8, 128), I32),
        ),
        in_specs=[pl.BlockSpec(memory_space=pltpu.HBM)] * 4,
        out_specs=tuple(pl.BlockSpec(memory_space=vmem) for n in range(5)),
        scratch_shapes=[
            vmem((4, 2, 4, 4, 8, 128), F32),
            vmem((4, 2, 4, 4, 16, 128), F32),
            vmem((4, 2, 4, 4, 16, 128), F32),
            vmem((512, 128), F32),
            vmem((512, 128), F32),
            vmem((31, 62), F32),
            vmem((31, 62), F32),
            vmem((16, 32), I32),
            vmem((32,), I32),
            vmem((16, 128), F32),
            vmem((16, 128), F32),
            vmem((8, 128), F32),
            vmem((16, 256), I32),
            dma((7,)),
            dma((3, 2)),
            dma((3,)),
            dma((3,)),
            dma((3, 4)),
            dma((3, 3)),
            dma((3, 4)),
        ],
        compiler_params=pltpu.CompilerParams(collective_id=0, has_side_effects=True, vmem_limit_bytes=16 << 20),
        name="gather",
    )(x, w, pos, cnt)


def tabled(*gathered):
    return pl.pallas_call(
        table_kernel,
        out_shape=jax.ShapeDtypeStruct((512, 256), F32),
        in_specs=[pl.BlockSpec(memory_space=pltpu.VMEM)] * 5,
        out_specs=pl.BlockSpec(memory_space=pl.ANY),
        scratch_shapes=[
            pltpu.SMEM((64, 128), I32),
            pltpu.SMEM((64, 128), I32),
            pltpu.SMEM((8, 128), I32),
            pltpu.VMEM((16416, 128), F32),
            pltpu.VMEM((256, 128), F32),
            pltpu.VMEM((1024, 128), F32),
            pltpu.SemaphoreType.DMA((3,)),
        ],
        compiler_params=pltpu.CompilerParams(vmem_limit_bytes=40 << 20),
        name="tables",
    )(*gathered)


def shards(moment_x, zinv, positions, entry_count):
    ins = (moment_x.T, zinv.T, positions.T, entry_count)
    return tabled(*gather(*(pltpu.with_memory_space_constraint(a, pltpu.HBM) for a in ins)))


def solution(mesh):
    return jax.shard_map(
        shards,
        mesh=mesh,
        in_specs=(P("row", "col"), P("row", "col"), P(("row", "col"), None), P(("row", "col"))),
        out_specs=P("row", "col"),
        check_vma=False,
    )
```
